32 devices in a mesh: dp: 4 (over z), seq: 4 (over y, x), tensor: 2 (over core).
Axes of the slice: x: 2, y: 2, z: 4, core: 2. Of those that a mesh axis runs over, the one named last changes fastest.
Arguments:
- hidden_in: float32 [2048, 1024], P(('dp', 'seq')), may hold values from -6 to 6
- cotangent: float32 [2048, 1024], P(('dp', 'seq')), may hold values from -6 to 6
- segment_ids: int32 [2048], P('dp'), may hold values from 0 to 3, as said below
- positions: int32 [2048], P('dp'), may hold values from 0 to 511, as said below
- w_query: bfloat16 [1024, 1024], P('dp', 'tensor'), may hold values from -0.1875 to 0.1875
- w_key: bfloat16 [1024, 256], P('dp', 'tensor'), may hold values from -0.1875 to 0.1875
- w_value: bfloat16 [1024, 256], P('dp', 'tensor'), may hold values from -0.1875 to 0.1875
- w_mamba_gate: bfloat16 [1024, 1536], P('dp', 'tensor'), may hold values from -0.1875 to 0.1875
- w_mamba_in: bfloat16 [1024, 1536], P('dp', 'tensor'), may hold values from -0.1875 to 0.1875
- w_mamba_bcdt: bfloat16 [1024, 280], P('dp'), may hold values from -0.1875 to 0.1875
- w_attention_out: bfloat16 [1024, 1024], P('tensor', 'dp'), may hold values from -0.5 to 0.5
- w_mamba_out: bfloat16 [1536, 1024], P('tensor', 'dp'), may hold values from -0.15625 to 0.15625
- w_feed_gate: bfloat16 [1024, 2048], P('dp', 'tensor'), may hold values from -0.1875 to 0.1875
- w_feed_up: bfloat16 [1024, 2048], P('dp', 'tensor'), may hold values from -0.1875 to 0.1875
- w_feed_down: bfloat16 [2048, 1024], P('tensor', 'dp'), may hold values from -0.125 to 0.125
- gain_mixer: bfloat16 [1024], P('dp'), may hold values from 0.5 to 1.5
- gain_feed: bfloat16 [1024], P('dp'), may hold values from 0.5 to 1.5
- conv_weight: float32 [4, 1792], replicated, may hold values from -0.6 to 0.6
- log_decay: float32 [24], replicated, may hold values from -3 to 0.7
- step_bias: float32 [24], replicated, may hold values from -5 to -3
- skip_scale: float32 [24], replicated, may hold values from 0.5 to 1.5
Outputs:
- output: float32 [2048, 1024], P(('dp', 'seq'))
- grad_hidden: float32 [2048, 1024], P(('dp', 'seq'))
- grad_w_query: float32 [1024, 1024], P('dp', 'tensor')
- grad_w_key: float32 [1024, 256], P('dp', 'tensor')
- grad_w_value: float32 [1024, 256], P('dp', 'tensor')
- grad_w_mamba_gate: float32 [1024, 1536], P('dp', 'tensor')
- grad_w_mamba_in: float32 [1024, 1536], P('dp', 'tensor')
- grad_w_mamba_bcdt: float32 [1024, 280], P('dp')
- grad_w_attention_out: float32 [1024, 1024], P('tensor', 'dp')
- grad_w_mamba_out: float32 [1536, 1024], P('tensor', 'dp')
- grad_w_feed_gate: float32 [1024, 2048], P('dp', 'tensor')
- grad_w_feed_up: float32 [1024, 2048], P('dp', 'tensor')
- grad_w_feed_down: float32 [2048, 1024], P('tensor', 'dp')
- grad_gain_mixer: float32 [1024], P('dp')
- grad_gain_feed: float32 [1024], P('dp')
- grad_conv_weight: float32 [4, 1792], replicated
- grad_log_decay: float32 [24], replicated
- grad_step_bias: float32 [24], replicated
- grad_skip_scale: float32 [24], replicated
The draws below stay inside these ranges and needn't reach their ends.
Inputs may be any that keep to these rules, and one draw needn't show every extreme that they name: `segment_ids`: within each aligned block of 512 tokens the ids number its sequences 0, 1, 2 ... in order; each sequence covers whole consecutive blocks of 128 tokens; the first run holds one sequence, the last run one sequence a block. `positions`: the index of each token within its sequence, counted from 0.
All inputs are finite; a program needn't handle non-finite values.
Results may differ from the reference program's by a relative error of at most 0.015.
Values may be sent and summed in bfloat16 or wider, within the bound.
A program may use at most 128 MiB of HBM per device.

```python
import functools
import math
import jax
import jax.numpy as jnp
from jax import lax

D = 1024
QH = 8
KVH = 2
HD = 128
MH = 24
MP = 64
NS = 128
KCONV = 4
FF = 2048
BLOCK = 128
MD = 1536
QCOL = 1024
KVCOL = 256
BCD = 280
CONVW = 1792
GROUP = 512
TOKENS = 2048
N_SEQ = 4
N_TENSOR = 2


def block_layout(key):
    base_key = jax.random.fold_in(key, 31)
    odds_key, cut_key = jax.random.split(base_key)
    group_count = TOKENS // GROUP
    block_count = GROUP // BLOCK
    cut_odds = jax.random.randint(odds_key, (group_count, 1), 0, 4)
    cut_draws = jax.random.randint(cut_key, (group_count, block_count), 0, 4)
    cut_flags = (cut_draws < cut_odds).astype(jnp.int32)
    group_index = jnp.arange(group_count, dtype=jnp.int32)[:, None]
    block_index = jnp.arange(block_count, dtype=jnp.int32)[None, :]
    cut_flags = jnp.where(group_index == group_count - 1, 1, cut_flags)
    cut_flags = jnp.where(group_index == 0, 0, cut_flags)
    cut_flags = jnp.where(block_index == 0, 1, cut_flags)
    sequence = jnp.cumsum(cut_flags, axis=1) - 1
    seq_start = lax.cummax(jnp.where(cut_flags == 1, block_index, 0), axis=1)
    offset = jnp.arange(BLOCK, dtype=jnp.int32)
    token_seq = jnp.repeat(sequence, BLOCK, axis=1).reshape(TOKENS)
    token_pos = ((block_index - seq_start)[:, :, None] * BLOCK + offset[None, None, :]).reshape(TOKENS)
    return (token_seq.astype(jnp.int32), token_pos.astype(jnp.int32))


def draw_segment_ids(key, part):
    return block_layout(key)[0]


def draw_positions(key, part):
    return block_layout(key)[1]


def steps_of(key, shape, cuts, low, largest):
    level, own = 1.0, jax.random.fold_in(key, 6)
    for axis_at, blocks in cuts:
        draws = jnp.exp(jax.random.uniform(jax.random.fold_in(own, axis_at), (blocks,), jnp.float32, low / len(cuts), largest / len(cuts)))
        level = level * jnp.repeat(draws, shape[axis_at] // blocks).reshape([-1 if axis == axis_at else 1 for axis in range(len(shape))])
    return level


def normal_values(stream_key, dims, spread, bound, pieces=(), kind=jnp.bfloat16):
    array = spread * jax.random.normal(stream_key, dims, jnp.float32)
    if pieces:
        array = array * steps_of(stream_key, dims, pieces, -0.22, 0.18)
    return jnp.clip(array, -bound, bound).astype(kind)


def setup_inputs(seed: int = 0) -> dict:
    splits = jax.random.split(jax.random.key(seed), 22)
    hidden_in = normal_values(splits[0], (TOKENS, D), 1.0, 6.0, ((0, 16),), jnp.float32)
    cotangent = normal_values(splits[1], (TOKENS, D), 1.0, 6.0, ((0, 16),), jnp.float32)
    segment_ids = draw_segment_ids(jax.random.fold_in(splits[21], 71), 0)
    positions = draw_positions(jax.random.fold_in(splits[21], 71), 0)
    w_query = normal_values(splits[4], (D, QCOL), D ** -0.5, 0.1875, ((0, 4), (1, 2)))
    w_key = normal_values(splits[5], (D, KVCOL), D ** -0.5, 0.1875, ((0, 4), (1, 2)))
    w_value = normal_values(splits[6], (D, KVCOL), D ** -0.5, 0.1875, ((0, 4), (1, 2)))
    w_mamba_gate = normal_values(splits[7], (D, MD), D ** -0.5, 0.1875, ((0, 4), (1, 2)))
    w_mamba_in = normal_values(splits[8], (D, MD), D ** -0.5, 0.1875, ((0, 4), (1, 2)))
    w_mamba_bcdt = normal_values(splits[9], (D, BCD), D ** -0.5, 0.1875, ((0, 4),))
    w_attention_out = normal_values(splits[10], (QCOL, D), HD ** -0.5, 0.5, ((0, 2), (1, 4)))
    w_mamba_out = normal_values(splits[11], (MD, D), MD ** -0.5, 0.15625, ((0, 2), (1, 4)))
    w_feed_gate = normal_values(splits[12], (D, FF), D ** -0.5, 0.1875, ((0, 4), (1, 2)))
    w_feed_up = normal_values(splits[13], (D, FF), D ** -0.5, 0.1875, ((0, 4), (1, 2)))
    w_feed_down = normal_values(splits[14], (FF, D), FF ** -0.5, 0.125, ((0, 2), (1, 4)))
    gain_mixer = jnp.clip(1.0 + 0.1 * jax.random.normal(splits[15], (D,), jnp.float32), 0.5, 1.5).astype(jnp.bfloat16)
    gain_feed = jnp.clip(1.0 + 0.1 * jax.random.normal(splits[16], (D,), jnp.float32), 0.5, 1.5).astype(jnp.bfloat16)
    conv_weight = jnp.clip(jax.random.uniform(splits[17], (KCONV, CONVW), jnp.float32, -0.6, 0.6), -0.6, 0.6)
    log_decay = jnp.clip(jax.random.uniform(splits[18], (MH,), jnp.float32, -3.0, 0.7), -3.0, 0.7)
    step_bias = jnp.clip(jax.random.uniform(splits[19], (MH,), jnp.float32, -5.0, -3.0), -5.0, -3.0)
    skip_scale = jnp.clip(jax.random.uniform(splits[20], (MH,), jnp.float32, 0.5, 1.5), 0.5, 1.5)
    return dict(hidden_in=hidden_in, cotangent=cotangent, segment_ids=segment_ids, positions=positions, w_query=w_query, w_key=w_key, w_value=w_value, w_mamba_gate=w_mamba_gate, w_mamba_in=w_mamba_in, w_mamba_bcdt=w_mamba_bcdt, w_attention_out=w_attention_out, w_mamba_out=w_mamba_out, w_feed_gate=w_feed_gate, w_feed_up=w_feed_up, w_feed_down=w_feed_down, gain_mixer=gain_mixer, gain_feed=gain_feed, conv_weight=conv_weight, log_decay=log_decay, step_bias=step_bias, skip_scale=skip_scale)


epsilon = 1e-05
rope_base = 100000000000.0
masked_score = -1e+30
highest = lax.Precision.HIGHEST

def matmul(left_in, right_in):
    return jnp.dot(left_in, right_in, preferred_element_type=jnp.float32)

def outer_product(left_in, right_in):
    return jnp.einsum('tc,td->cd', left_in, right_in, preferred_element_type=jnp.float32)

def back_product(grad_in, weight_in):
    return jnp.einsum('tc,dc->td', grad_in, weight_in, preferred_element_type=jnp.float32)

def rope_angles(token_pos, head_width):
    half_width = head_width // 2
    freq_index = jnp.arange(half_width, dtype=jnp.float32)
    inverse_freq = jnp.exp(freq_index * (-2.0 * math.log(rope_base) / head_width))
    angles = token_pos.astype(jnp.float32)[:, None] * inverse_freq[None, :]
    return (jnp.cos(angles), jnp.sin(angles))

def rotate(values, cosine, sine_vals):
    half_width = values.shape[-1] // 2
    first_half = values[..., :half_width]
    second_half = values[..., half_width:]
    cos_rows = cosine[:, None, :]
    sin_rows = sine_vals[:, None, :]
    return jnp.concatenate([first_half * cos_rows - second_half * sin_rows, second_half * cos_rows + first_half * sin_rows], axis=-1)

def rms_forward(values, gain_vec):
    scale_rows = lax.rsqrt(lax.optimization_barrier(jnp.mean(values * values, axis=1, keepdims=True)) + epsilon)
    normed = values * scale_rows
    return (normed, scale_rows, (normed * gain_vec.astype(jnp.float32)[None, :]).astype(jnp.bfloat16))

def rms_backward(grad_out, normed, scale_rows, gain_vec, upstream):
    grad_gain = lax.optimization_barrier(jnp.sum(grad_out * normed, axis=0))
    grad_normed = grad_out * gain_vec.astype(jnp.float32)[None, :]
    grad_in = upstream + scale_rows * (grad_normed - normed * lax.optimization_barrier(jnp.mean(grad_normed * normed, axis=1, keepdims=True)))
    return (grad_in, grad_gain)

def silu_slope(pre_act):
    sigmoid_gate = jax.nn.sigmoid(pre_act)
    return sigmoid_gate * (1.0 + pre_act * (1.0 - sigmoid_gate))

def attend_forward(query_in, key_in, value_in, allowed, score_scale):
    total_rows = query_in.shape[0]
    block_rows = min(total_rows, 512)
    block_count = total_rows // block_rows

    def one_block(block_index):
        row_start = block_index * block_rows
        query_rows = lax.dynamic_slice_in_dim(query_in, row_start, block_rows, 0)
        visible = lax.dynamic_slice_in_dim(allowed, row_start, block_rows, 0)
        scores = jnp.einsum('qd,kd->qk', query_rows, key_in, preferred_element_type=jnp.float32) * score_scale
        scores = jnp.where(visible, scores, masked_score)
        row_peak = lax.optimization_barrier(jnp.max(scores, axis=1, keepdims=True))
        logsum = row_peak + jnp.log(lax.optimization_barrier(jnp.sum(jnp.exp(scores - row_peak), axis=1, keepdims=True)))
        softmax_low = jnp.exp(scores - logsum).astype(jnp.bfloat16)
        result = jnp.dot(softmax_low, value_in, preferred_element_type=jnp.float32).astype(jnp.bfloat16)
        return (result, logsum[:, 0])
    result, logsum = lax.map(one_block, jnp.arange(block_count, dtype=jnp.int32))
    return (result.reshape(total_rows, value_in.shape[1]), logsum.reshape(total_rows))

def attend_backward(query_in, key_in, value_in, allowed, score_scale, result, logsum, grad_result):
    total_rows, head_width = query_in.shape
    block_rows = min(total_rows, 512)
    block_count = total_rows // block_rows
    row_delta = lax.optimization_barrier(jnp.sum(grad_result.astype(jnp.float32) * result.astype(jnp.float32), axis=1))

    def one_block(totals, block_index):
        grad_key, grad_value = totals
        row_start = block_index * block_rows
        query_rows = lax.dynamic_slice_in_dim(query_in, row_start, block_rows, 0)
        visible = lax.dynamic_slice_in_dim(allowed, row_start, block_rows, 0)
        grad_rows = lax.dynamic_slice_in_dim(grad_result, row_start, block_rows, 0)
        logsum_rows = lax.dynamic_slice_in_dim(logsum, row_start, block_rows, 0)
        delta_rows = lax.dynamic_slice_in_dim(row_delta, row_start, block_rows, 0)
        scores = jnp.einsum('qd,kd->qk', query_rows, key_in, preferred_element_type=jnp.float32) * score_scale
        scores = jnp.where(visible, scores, masked_score)
        softmax_f = jnp.exp(scores - logsum_rows[:, None])
        grad_value = grad_value + jnp.einsum('qk,qd->kd', softmax_f.astype(jnp.bfloat16), grad_rows, preferred_element_type=jnp.float32)
        grad_probs = jnp.einsum('qd,kd->qk', grad_rows, value_in, preferred_element_type=jnp.float32)
        grad_scores = (softmax_f * (grad_probs - delta_rows[:, None])).astype(jnp.bfloat16)
        grad_query = jnp.dot(grad_scores, key_in, preferred_element_type=jnp.float32) * score_scale
        grad_key = grad_key + jnp.einsum('qk,qd->kd', grad_scores, query_rows, preferred_element_type=jnp.float32) * score_scale
        return ((grad_key, grad_value), grad_query)
    zero_rows = jnp.zeros((total_rows, head_width), jnp.float32)
    (grad_key, grad_value), grad_query = lax.scan(one_block, (zero_rows, zero_rows), jnp.arange(block_count, dtype=jnp.int32))
    return (grad_query.reshape(total_rows, head_width), grad_key, grad_value)

def mamba_core(mixed_in, step_raw, conv_taps, log_rate, bias_step, skip_gain, segment_ids, allowed):
    total_rows, col_width = mixed_in.shape
    head_count = step_raw.shape[1]
    conv_sum = conv_taps[0][None, :] * mixed_in
    for shift_lag in range(1, conv_taps.shape[0]):
        shifted = jnp.concatenate([jnp.zeros((shift_lag, col_width), mixed_in.dtype), mixed_in[:-shift_lag]], axis=0)
        same_seq = jnp.concatenate([jnp.zeros((shift_lag,), dtype=bool), segment_ids[shift_lag:] == segment_ids[:-shift_lag]], axis=0)
        conv_sum = conv_sum + conv_taps[shift_lag][None, :] * jnp.where(same_seq[:, None], shifted, 0.0)
    activated = jax.nn.silu(conv_sum)
    head_in = activated[:, :head_count * MP].reshape(total_rows, head_count, MP)
    state_in = activated[:, head_count * MP:head_count * MP + NS]
    state_out = activated[:, head_count * MP + NS:]
    step_size = jax.nn.softplus(step_raw + bias_step[None, :])
    log_rates = -step_size * jnp.exp(log_rate)[None, :]
    cumulative = jnp.cumsum(log_rates, axis=0).T
    intersection = jnp.dot(state_out, state_in.T, precision=highest)
    log_gap = cumulative[:, :, None] - cumulative[:, None, :]
    decay_mat = jnp.exp(jnp.where(allowed[None, :, :], log_gap, masked_score))
    mixing = intersection[None, :, :] * decay_mat * step_size.T[:, None, :]
    result = jnp.einsum('hts,shp->thp', mixing, head_in, precision=highest) + skip_gain[None, :, None] * head_in
    return result.reshape(total_rows, head_count * MP)

def layer_group(params, hidden_in, cotangent, segment_ids, positions):
    w_query, w_key, w_value, w_mamba_gate, w_mamba_in, w_mamba_bcdt, w_attention_out, w_mamba_out, w_feed_gate, w_feed_up, w_feed_down, gain_mixer, gain_feed, conv_weight, log_decay, step_bias, skip_scale = params
    length = hidden_in.shape[0]
    dev_groups = N_SEQ * N_TENSOR
    heads_dev = MH // dev_groups
    mamba_width = heads_dev * MP
    score_scale = HD ** (-0.5)
    allowed = (segment_ids[:, None] == segment_ids[None, :]) & (positions[None, :] <= positions[:, None])
    cosine, sine_vals = rope_angles(positions, HD)
    core = functools.partial(mamba_core, segment_ids=segment_ids, allowed=allowed)
    normed_one, scale_one, mixer_in = rms_forward(hidden_in, gain_mixer)
    query_all = rotate(matmul(mixer_in, w_query).reshape(length, QH, HD), cosine, sine_vals).astype(jnp.bfloat16).transpose(1, 0, 2)
    key_all = rotate(matmul(mixer_in, w_key).reshape(length, KVH, HD), cosine, sine_vals).astype(jnp.bfloat16).transpose(1, 0, 2)
    value_all = matmul(mixer_in, w_value).reshape(length, KVH, HD).astype(jnp.bfloat16).transpose(1, 0, 2)
    gate_pre = matmul(mixer_in, w_mamba_gate)
    mamba_low = matmul(mixer_in, w_mamba_in).astype(jnp.bfloat16)
    bcdt_low = matmul(mixer_in, w_mamba_bcdt).astype(jnp.bfloat16)

    def device_inputs(group_index):
        x_cols = lax.dynamic_slice_in_dim(mamba_low, group_index * mamba_width, mamba_width, 1)
        mixed_in = jnp.concatenate([x_cols, bcdt_low[:, :2 * NS]], axis=1).astype(jnp.float32)
        step_raw = lax.dynamic_slice_in_dim(bcdt_low, 2 * NS + group_index * heads_dev, heads_dev, 1).astype(jnp.float32)
        conv_taps = jnp.concatenate([lax.dynamic_slice_in_dim(conv_weight, group_index * mamba_width, mamba_width, 1), conv_weight[:, MD:]], axis=1)
        log_rate = lax.dynamic_slice_in_dim(log_decay, group_index * heads_dev, heads_dev, 0)
        bias_step = lax.dynamic_slice_in_dim(step_bias, group_index * heads_dev, heads_dev, 0)
        skip_gain = lax.dynamic_slice_in_dim(skip_scale, group_index * heads_dev, heads_dev, 0)
        return (mixed_in, step_raw, conv_taps, log_rate, bias_step, skip_gain)

    def forward_one(group_index):
        attended, logsum = attend_forward(query_all[group_index], key_all[group_index // N_SEQ], value_all[group_index // N_SEQ], allowed, score_scale)
        ssm_low = core(*device_inputs(group_index)).astype(jnp.bfloat16)
        return (attended, logsum, ssm_low)
    group_ids = jnp.arange(dev_groups, dtype=jnp.int32)
    attended_all, logsum_all, ssm_all = lax.map(forward_one, group_ids)
    attention_cat = attended_all.transpose(1, 0, 2).reshape(length, QCOL)
    ssm_cat = ssm_all.transpose(1, 0, 2).reshape(length, MD)
    silu_gate = jax.nn.silu(gate_pre)
    gated = (ssm_cat.astype(jnp.float32) * silu_gate).astype(jnp.bfloat16)
    middle = hidden_in + (matmul(attention_cat, w_attention_out) + matmul(gated, w_mamba_out))
    normed_two, scale_two, feed_in = rms_forward(middle, gain_feed)
    feed_gate = matmul(feed_in, w_feed_gate)
    feed_up = matmul(feed_in, w_feed_up)
    activated = (jax.nn.silu(feed_gate) * feed_up).astype(jnp.bfloat16)
    output = middle + matmul(activated, w_feed_down)
    cot_low = cotangent.astype(jnp.bfloat16)
    grad_w_feed_down = outer_product(activated, cot_low)
    grad_act = back_product(cot_low, w_feed_down)
    grad_feed_gate_in = (grad_act * feed_up * silu_slope(feed_gate)).astype(jnp.bfloat16)
    grad_feed_up_in = (grad_act * jax.nn.silu(feed_gate)).astype(jnp.bfloat16)
    grad_w_feed_gate = outer_product(feed_in, grad_feed_gate_in)
    grad_w_feed_up = outer_product(feed_in, grad_feed_up_in)
    grad_feed_in = back_product(grad_feed_gate_in, w_feed_gate) + back_product(grad_feed_up_in, w_feed_up)
    grad_middle, grad_gain_feed = rms_backward(grad_feed_in, normed_two, scale_two, gain_feed, cotangent)
    middle_low = grad_middle.astype(jnp.bfloat16)
    grad_w_attention_out = outer_product(attention_cat, middle_low)
    grad_w_mamba_out = outer_product(gated, middle_low)
    grad_gated = back_product(middle_low, w_mamba_out)
    grad_attended = back_product(middle_low, w_attention_out).astype(jnp.bfloat16)
    grad_ssm = (grad_gated * silu_gate).astype(jnp.bfloat16)
    grad_gate_in = (grad_gated * ssm_cat.astype(jnp.float32) * silu_slope(gate_pre)).astype(jnp.bfloat16)
    grad_att_heads = grad_attended.reshape(length, QH, HD).transpose(1, 0, 2)
    grad_ssm_heads = grad_ssm.reshape(length, dev_groups, mamba_width).transpose(1, 0, 2)

    def backward_one(group_index):
        key_in = key_all[group_index // N_SEQ]
        value_in = value_all[group_index // N_SEQ]
        query_in = query_all[group_index]
        grad_query, grad_key, grad_value = attend_backward(query_in, key_in, value_in, allowed, score_scale, attended_all[group_index], logsum_all[group_index], grad_att_heads[group_index])
        query_low = rotate(grad_query[:, None, :], cosine, -sine_vals)[:, 0, :].astype(jnp.bfloat16)
        key_low = rotate(grad_key[:, None, :], cosine, -sine_vals)[:, 0, :].astype(jnp.bfloat16)
        value_low = grad_value.astype(jnp.bfloat16)
        core_out, pullback = jax.vjp(core, *device_inputs(group_index))
        core_grads = pullback(grad_ssm_heads[group_index].astype(jnp.float32))
        return (query_low, key_low, value_low, core_grads[0].astype(jnp.bfloat16), core_grads[1].astype(jnp.bfloat16), core_grads[2], core_grads[3], core_grads[4], core_grads[5])
    dq_all, dk_all, dv_all, dmix_all, dstep_all, dconv_all, drate_all, dbias_all, dskip_all = lax.map(backward_one, group_ids)
    dq_low = dq_all.transpose(1, 0, 2).reshape(length, QCOL)
    dk_low = lax.optimization_barrier(jnp.sum(dk_all.astype(jnp.float32).reshape(KVH, N_SEQ, length, HD), axis=1)).transpose(1, 0, 2).reshape(length, KVCOL).astype(jnp.bfloat16)
    dv_low = lax.optimization_barrier(jnp.sum(dv_all.astype(jnp.float32).reshape(KVH, N_SEQ, length, HD), axis=1)).transpose(1, 0, 2).reshape(length, KVCOL).astype(jnp.bfloat16)
    dx_low = dmix_all[:, :, :mamba_width].transpose(1, 0, 2).reshape(length, MD)
    dstate = lax.optimization_barrier(jnp.sum(dmix_all[:, :, mamba_width:].astype(jnp.float32), axis=0))
    dstep = dstep_all.transpose(1, 0, 2).reshape(length, MH).astype(jnp.float32)
    dbcdt_low = jnp.concatenate([dstate, dstep], axis=1).astype(jnp.bfloat16)
    grad_conv_weight = jnp.concatenate([dconv_all[:, :, :mamba_width].transpose(1, 0, 2).reshape(KCONV, MD), lax.optimization_barrier(jnp.sum(dconv_all[:, :, mamba_width:], axis=0))], axis=1)
    grad_log_decay = drate_all.reshape(MH)
    grad_step_bias = dbias_all.reshape(MH)
    grad_skip_scale = dskip_all.reshape(MH)
    grad_w_query = outer_product(mixer_in, dq_low)
    grad_w_key = outer_product(mixer_in, dk_low)
    grad_w_value = outer_product(mixer_in, dv_low)
    grad_w_mamba_gate = outer_product(mixer_in, grad_gate_in)
    grad_w_mamba_in = outer_product(mixer_in, dx_low)
    grad_w_mamba_bcdt = outer_product(mixer_in, dbcdt_low)
    grad_mixer_in = back_product(dq_low, w_query) + back_product(dk_low, w_key) + back_product(dv_low, w_value) + back_product(grad_gate_in, w_mamba_gate) + back_product(dx_low, w_mamba_in) + back_product(dbcdt_low, w_mamba_bcdt)
    grad_hidden, grad_gain_mixer = rms_backward(grad_mixer_in, normed_one, scale_one, gain_mixer, grad_middle)
    grads = (grad_w_query, grad_w_key, grad_w_value, grad_w_mamba_gate, grad_w_mamba_in, grad_w_mamba_bcdt, grad_w_attention_out, grad_w_mamba_out, grad_w_feed_gate, grad_w_feed_up, grad_w_feed_down, grad_gain_mixer, grad_gain_feed, grad_conv_weight, grad_log_decay, grad_step_bias, grad_skip_scale)
    return (output, grad_hidden, grads)

def reference(hidden_in, cotangent, segment_ids, positions, w_query, w_key, w_value, w_mamba_gate, w_mamba_in, w_mamba_bcdt, w_attention_out, w_mamba_out, w_feed_gate, w_feed_up, w_feed_down, gain_mixer, gain_feed, conv_weight, log_decay, step_bias, skip_scale):
    params = (w_query, w_key, w_value, w_mamba_gate, w_mamba_in, w_mamba_bcdt, w_attention_out, w_mamba_out, w_feed_gate, w_feed_up, w_feed_down, gain_mixer, gain_feed, conv_weight, log_decay, step_bias, skip_scale)
    group_count = hidden_in.shape[0] // GROUP
    stacked = (hidden_in.reshape(group_count, GROUP, D), cotangent.reshape(group_count, GROUP, D), segment_ids.reshape(group_count, GROUP), positions.reshape(group_count, GROUP))
    zero_grads = jax.tree.map(lambda weight_arr: jnp.zeros(weight_arr.shape, jnp.float32), params)

    def scan_group(totals, inputs):
        output, grad_hidden, grads = layer_group(params, inputs[0], inputs[1], inputs[2], inputs[3])
        return (jax.tree.map(lambda left_sum, right_sum: left_sum + right_sum, totals, grads), (output, grad_hidden))
    totals, (output, grad_hidden) = lax.scan(scan_group, zero_grads, stacked)
    return (output.reshape(group_count * GROUP, D), grad_hidden.reshape(group_count * GROUP, D), totals[0], totals[1], totals[2], totals[3], totals[4], totals[5], totals[6], totals[7], totals[8], totals[9], totals[10], totals[11], totals[12], totals[13], totals[14], totals[15], totals[16])
```

```python
import functools
import math

import jax
import jax.numpy as jnp
from jax import lax
from jax.experimental import pallas as pl
from jax.experimental.pallas import tpu as pltpu
from jax.sharding import PartitionSpec as P

D = 1024
HD = 128
MH = 24
MP = 64
NS = 128
KCONV = 4
MD = 1536

MESH = pl.DeviceIdType.MESH
LOW = jnp.bfloat16
F32 = jnp.float32

epsilon = 1e-05
rope_base = 100000000000.0
masked_score = -1e30
highest = lax.Precision.HIGHEST


def ring_order(axis):
    count = lax.axis_size(axis)
    return [0, 1, 3, 2] if axis == "seq" and count == 4 else list(range(count))


def ring_place(axis):
    index = lax.axis_index(axis)
    if axis == "seq" and lax.axis_size(axis) == 4:
        return index + (index // 2) * (1 - 2 * (index % 2))
    return index


def hop(value, axis, step):
    order = ring_order(axis)
    count = len(order)
    return lax.ppermute(value, axis, [(order[i], order[(i + step) % count]) for i in range(count)])


def ring_gather(block, axis):
    order = ring_order(axis)
    count = len(order)
    half = block.shape[0] // 2
    by_offset = {0: block}
    right = left = block
    for step in range(1, count // 2):
        right, left = hop(right, axis, 1), hop(left, axis, -1)
        by_offset[step], by_offset[count - step] = right, left
    by_offset[count // 2] = jnp.concatenate(
        [hop(right[:half], axis, 1), hop(left[half:], axis, -1)], axis=0
    )
    stack = jnp.stack([by_offset[o] for o in range(count)])
    place = ring_place(axis)
    places = {index: p for p, index in enumerate(order)}
    return [
        lax.dynamic_index_in_dim(stack, lax.rem(place - places[i] + count, count), 0, keepdims=False)
        for i in range(count)
    ]


def ring_scatter(whole, axis, dim):
    count = lax.axis_size(axis)
    size = whole.shape[dim] // count
    me = lax.axis_index(axis)

    def part(offset):
        return lax.dynamic_slice_in_dim(
            whole, lax.rem(me + offset + count, count) * size, size, dim
        )

    far = count // 2
    first = part(far)
    half = first.shape[0] // 2
    right = hop(first[:half].astype(LOW), axis, 1).astype(F32)
    left = hop(first[half:].astype(LOW), axis, -1).astype(F32)
    for step in range(far - 1, -1, -1):
        mine_right, mine_left = part(step), part(-step)
        if step == far - 1:
            new_right = jnp.concatenate([mine_right[:half] + right, mine_right[half:]], axis=0)
            new_left = jnp.concatenate([mine_left[:half], mine_left[half:] + left], axis=0)
        else:
            new_right, new_left = mine_right + right, mine_left + left
        if step == 0:
            if far == 1:
                return jnp.concatenate([mine_right[:half] + right, mine_left[half:] + left], axis=0)
            return mine_right + right + left
        right = hop(new_right.astype(LOW), axis, 1).astype(F32)
        left = hop(new_left.astype(LOW), axis, -1).astype(F32)


def seq_partner(seq_index, k):
    if k == 1:
        return seq_index + 1 - 2 * (seq_index % 2)
    if k == 2:
        return seq_index + 2 - 4 * (seq_index // 2)
    return 3 - seq_index


def greet(devices):
    barrier = pltpu.get_barrier_semaphore()
    for device in devices:
        pl.semaphore_signal(barrier, inc=1, device_id=device, device_id_type=MESH)
    pl.semaphore_wait(barrier, len(devices))


def plane_peers():
    s, t = lax.axis_index("seq"), lax.axis_index("tensor")
    return [{"seq": seq_partner(s, k), "tensor": t} for k in (1, 2, 3)] + [
        {"seq": s, "tensor": 1 - t}
    ]


def send(src, dst, send_sem, recv_sem, device):
    copy = pltpu.make_async_remote_copy(
        src_ref=src,
        dst_ref=dst,
        send_sem=send_sem,
        recv_sem=recv_sem,
        device_id=device,
        device_id_type=MESH,
    )
    copy.start()
    return copy


def spread_rows(out_ref, rows, send_sem, recv_sem):
    s, t = lax.axis_index("seq"), lax.axis_index("tensor")
    other = {"seq": s, "tensor": 1 - t}
    mine = out_ref.at[pl.ds(pl.multiple_of((2 * s + t) * rows, rows), rows)]
    copies = [
        send(mine, mine, send_sem.at[k], recv_sem.at[k], {"seq": seq_partner(s, k), "tensor": t})
        for k in (1, 2, 3)
    ]
    copies.append(send(mine, mine, send_sem.at[0], recv_sem.at[0], other))
    for k in (1, 2, 3):
        copies[k - 1].wait_recv()
        came = out_ref.at[pl.ds(pl.multiple_of((2 * seq_partner(s, k) + t) * rows, rows), rows)]
        copies.append(send(came, came, send_sem.at[3 + k], recv_sem.at[3 + k], other))
    for copy in copies[3:]:
        copy.wait_recv()
    for copy in copies:
        copy.wait_send()


def sum_rows(part_ref, near_ref, out_low_ref, far_ref, send_sem, recv_sem):
    s, t = lax.axis_index("seq"), lax.axis_index("tensor")
    other = {"seq": s, "tensor": 1 - t}
    to = [s, seq_partner(s, 1), seq_partner(s, 2), seq_partner(s, 3)]
    near = {
        k: send(part_ref.at[to[k], 1 - t], near_ref.at[k], send_sem.at[k], recv_sem.at[k], other)
        for k in (3, 1, 2, 0)
    }
    far = {}
    for k in (3, 1, 2):
        near[k].wait_recv()
        out_low_ref[k] = (part_ref[to[k], t].astype(F32) + near_ref[k].astype(F32)).astype(LOW)
        far[k] = send(
            out_low_ref.at[k],
            far_ref.at[k],
            send_sem.at[4 + k],
            recv_sem.at[4 + k],
            {"seq": to[k], "tensor": t},
        )
    near[0].wait_recv()
    total = part_ref[s, t].astype(F32) + near_ref[0].astype(F32)
    for k in (1, 2, 3):
        far[k].wait_recv()
        total = total + far_ref[k].astype(F32)
    for copy in (*near.values(), *far.values()):
        copy.wait_send()
    return total


def dot_nt(left, right, precision=None):
    return lax.dot_general(left, right, (((1,), (1,)), ((), ())), precision=precision, preferred_element_type=F32)


def dot_tn(left, right, precision=None):
    return lax.dot_general(left, right, (((0,), (0,)), ((), ())), precision=precision, preferred_element_type=F32)


def dot_nn(left, right, precision=None):
    return lax.dot_general(left, right, (((1,), (0,)), ((), ())), precision=precision, preferred_element_type=F32)


def turn(values, cos_ref, sin_ref):
    return values * cos_ref[...] + pltpu.roll(values, HD // 2, 1) * sin_ref[...]


def turn_back(values, cos_ref, sin_ref):
    return values * cos_ref[...] - pltpu.roll(values, HD // 2, 1) * sin_ref[...]


def visible(col_ref, row_ref):
    return (col_ref[:, 0:1] == row_ref[0:1, :]) & (row_ref[1:2, :] <= col_ref[:, 1:2])


def convolve(mixed, taps_ref, col_ref):
    total = taps_ref[0:1] * mixed
    for lag in range(1, KCONV):
        kept = jnp.where(col_ref[:, 1:2] >= lag, pltpu.roll(mixed, lag, 0), 0.0)
        total = total + taps_ref[lag : lag + 1] * kept
    return total


def steps_and_sums(raw, head_ref, heads):
    raw = jnp.where(lax.broadcasted_iota(jnp.int32, raw.shape, 0) < heads, raw, 0.0)
    pre = raw + head_ref[:, 0:1]
    step = jnp.maximum(pre, 0.0) + jnp.log1p(jnp.exp(-jnp.abs(pre)))
    rate = -step * jnp.exp(head_ref[:, 1:2])
    length = raw.shape[1]
    upto = lax.broadcasted_iota(jnp.int32, (length, length), 0) <= lax.broadcasted_iota(
        jnp.int32, (length, length), 1
    )
    return pre, step, rate, dot_nn(rate, upto.astype(F32), highest)


def dp_sends(dp_count, src, dst_of, sems, row):
    d = lax.axis_index("dp")
    return [
        send(src, dst_of(k), sems.at[row, k], sems.at[row + 1, k], {"dp": lax.rem(d + k, dp_count)})
        for k in range(1, dp_count)
    ]


def forward_kernel(
    dp_count, heads,
    spare_ref, hid_ref, cot_ref, entry_own, feed_own, outs_own, cos_ref, sin_ref, col_ref, row_ref, taps_ref, head_ref,
    spare_out, tok_ref, entry_w, feed_w, outs_w, kv_ref, query_out, gate_out, x_out, step_out, mixed_ref, ssm_out,
    logsum_out, middle_ref, feed_ref,
    came, part, near, low, far, sems, local, ss, rs, s2, r2, s3, r3, s4, r4,
):
    d, s, t = lax.axis_index("dp"), lax.axis_index("seq"), lax.axis_index("tensor")
    rows, owner, width = hid_ref.shape[0], entry_own.shape[0], heads * MP
    length = tok_ref.shape[0]
    greet(plane_peers() + [{"dp": lax.rem(d + k, dp_count)} for k in range(1, dp_count)])
    place = pl.ds(pl.multiple_of(d * owner, owner), owner)
    spares = dp_sends(dp_count, spare_ref, lambda k: came.at[k], sems, 0)
    entries = dp_sends(dp_count, entry_own, lambda k: entry_w.at[place], sems, 2)
    locals_ = [
        pltpu.make_async_copy(own, full.at[place], local.at[i])
        for i, (own, full) in enumerate(((entry_own, entry_w), (feed_own, feed_w), (outs_own, outs_w)))
    ]
    for copy in locals_:
        copy.start()
    hid = hid_ref[...]
    normed = hid * lax.rsqrt(jnp.mean(hid * hid, axis=1, keepdims=True) + epsilon)
    total = spare_ref[...]
    for k in range(1, dp_count):
        spares[k - 1].wait_recv()
        total = total + came[k]
    spare_out[...] = total
    mine = pl.ds(pl.multiple_of((2 * s + t) * rows, rows), rows)
    tok_ref[mine, :D] = (normed * total[3:4]).astype(LOW)
    tok_ref[mine, D:] = cot_ref[...].astype(LOW)
    spread_rows(tok_ref, rows, ss, rs)
    for copy in entries:
        copy.wait_recv()
    outers = dp_sends(dp_count, outs_own, lambda k: outs_w.at[place], sems, 4)
    feeds = dp_sends(dp_count, feed_own, lambda k: feed_w.at[place], sems, 6)
    for copy in locals_:
        copy.wait()

    mixer_in = tok_ref[:, :D]
    aux = dot_nn(mixer_in, entry_w[:, HD : 2 * HD])
    is_key = jnp.where(s == 0, 1.0, 0.0)
    aux = turn(aux, cos_ref, sin_ref) * is_key + aux * (1.0 - is_key)
    kv_ref[s] = aux.astype(LOW)
    shared = [
        send(kv_ref.at[s], kv_ref.at[s], s4.at[k], r4.at[k], {"seq": seq_partner(s, k), "tensor": t})
        for k in (1, 2, 3)
    ]
    query = turn(dot_nn(mixer_in, entry_w[:, :HD]), cos_ref, sin_ref).astype(LOW)
    query_out[...] = query
    gate_x = dot_nn(mixer_in, entry_w[:, 2 * HD :])
    gate_pre, x_low = gate_x[:, :width], gate_x[:, width:].astype(LOW)
    gate_out[...] = gate_pre
    x_out[...] = x_low
    step_low = dot_nt(total.astype(LOW), mixer_in).astype(LOW).astype(F32)
    step_out[...] = step_low
    _, step, _, cum = steps_and_sums(step_low, head_ref, heads)
    cum_col = cum.T
    x_act = convolve(x_low.astype(F32), taps_ref.at[:, 2 * NS :], col_ref)
    x_act = x_act * jax.nn.sigmoid(x_act)
    allowed = visible(col_ref, row_ref)
    for copy in shared:
        copy.wait_recv()

    scores = jnp.where(allowed, dot_nt(query, kv_ref[0]) * HD ** (-0.5), masked_score)
    peak = jnp.max(scores, axis=1, keepdims=True)
    logsum = peak + jnp.log(jnp.sum(jnp.exp(scores - peak), axis=1, keepdims=True))
    logsum_out[...] = logsum
    attended = dot_nn(jnp.exp(scores - logsum).astype(LOW), kv_ref[1]).astype(LOW)
    mixed_ref[:, :HD] = attended

    bstate = convolve(kv_ref[2].astype(F32), taps_ref.at[:, :NS], col_ref)
    bstate = bstate * jax.nn.sigmoid(bstate)
    cstate = convolve(kv_ref[3].astype(F32), taps_ref.at[:, NS : 2 * NS], col_ref)
    cstate = cstate * jax.nn.sigmoid(cstate)
    meet = dot_nt(cstate, bstate, highest)
    outs = []
    for h in range(heads):
        decay = jnp.exp(jnp.where(allowed, cum_col[:, h : h + 1] - cum[h : h + 1, :], masked_score))
        x_head = x_act[:, h * MP : (h + 1) * MP]
        outs.append(dot_nn(meet * decay * step[h : h + 1, :], x_head, highest) + head_ref[h : h + 1, 2:3] * x_head)
    ssm_low = jnp.concatenate(outs, axis=1).astype(LOW)
    ssm_out[...] = ssm_low
    gated = (ssm_low.astype(F32) * (gate_pre * jax.nn.sigmoid(gate_pre))).astype(LOW)
    mixed_ref[:, HD:] = gated

    for copy in outers:
        copy.wait_recv()
    part[...] = (
        dot_nt(attended, outs_w[:, :HD]) + dot_nt(gated, outs_w[:, HD : HD + width])
    ).astype(LOW).reshape(part.shape)
    middle = hid_ref[...] + sum_rows(part, near, low, far, s2, r2)
    middle_ref[...] = middle
    scale = lax.rsqrt(jnp.mean(middle * middle, axis=1, keepdims=True) + epsilon)
    feed_ref[mine, :] = (middle * scale * total[4:5]).astype(LOW)
    spread_rows(feed_ref, rows, s3, r3)
    for copy in feeds:
        copy.wait_recv()
    for copy in (*spares, *entries, *outers, *feeds, *shared):
        copy.wait_send()


def norm_backward(grad, values, gain, upstream):
    scale = lax.rsqrt(jnp.mean(values * values, axis=1, keepdims=True) + epsilon)
    normed = values * scale
    grad_gain = jnp.sum(grad * normed, axis=0, keepdims=True)
    inner = grad * gain
    result = upstream + scale * (inner - normed * jnp.mean(inner * normed, axis=1, keepdims=True))
    return result, grad_gain


def feed_back_kernel(
    part_ref, middle_ref, gain_ref, cot_ref, grad_ref, gain_out, low_out, near, low, far, s1, r1, s2, r2
):
    s, t = lax.axis_index("seq"), lax.axis_index("tensor")
    rows = middle_ref.shape[0]
    greet(plane_peers())
    total = sum_rows(part_ref, near, low, far, s1, r1)
    grad, grad_gain = norm_backward(total, middle_ref[...], gain_ref[4:5], cot_ref[...])
    grad_ref[...] = grad
    gain_out[...] = jnp.broadcast_to(grad_gain, gain_out.shape)
    mine = pl.ds(pl.multiple_of((2 * s + t) * rows, rows), rows)
    low_out[mine, :] = grad.astype(LOW)
    spread_rows(low_out, rows, s2, r2)


def last_kernel(
    part_a, part_b, middle_ref, hid_ref, gain_ref, grad_ref, out_a, out_b, gain_out,
    near_a, low_a, far_a, near_b, low_b, far_b, s1, r1, s2, r2, s3, r3,
):
    s, t = lax.axis_index("seq"), lax.axis_index("tensor")
    other = {"seq": s, "tensor": 1 - t}
    greet(plane_peers())
    total = sum_rows(part_b, near_b, low_b, far_b, s2, r2)
    grad, grad_gain = norm_backward(total, hid_ref[...], gain_ref[3:4], grad_ref[...])
    gain_out[...] = jnp.broadcast_to(grad_gain, gain_out.shape)
    out_b[t] = grad
    copy_b = send(out_b.at[t], out_b.at[t], s3.at[1], r3.at[1], other)
    out_a[t] = middle_ref[...] + sum_rows(part_a, near_a, low_a, far_a, s1, r1)
    copy_a = send(out_a.at[t], out_a.at[t], s3.at[0], r3.at[0], other)
    for copy in (copy_a, copy_b):
        copy.wait_recv()
        copy.wait_send()


def small_kernel(dp_count, own_ref, all_ref, came, sends, recvs, s2, r2):
    d, s, t = lax.axis_index("dp"), lax.axis_index("seq"), lax.axis_index("tensor")
    peers = []
    for k in range(4):
        for flip in range(2):
            if k or flip:
                to = s if k == 0 else seq_partner(s, k)
                peers.append({"seq": to, "tensor": 1 - t if flip else t})
    dp_peers = [{"dp": lax.rem(d + k, dp_count)} for k in range(1, dp_count)]
    greet(peers + dp_peers)
    copies = [
        send(own_ref, came.at[k], sends.at[k], recvs.at[k], dp_peers[k - 1])
        for k in range(1, dp_count)
    ]
    total = own_ref[...]
    for k in range(1, dp_count):
        copies[k - 1].wait_recv()
        total = total + came[k]
    mine = 2 * s + t
    all_ref[mine] = total
    later = [
        send(all_ref.at[mine], all_ref.at[mine], s2.at[i], r2.at[i], peer)
        for i, peer in enumerate(peers)
    ]
    for copy in later:
        copy.wait_recv()
    for copy in (*copies, *later):
        copy.wait_send()


def call(kernel, collective_id, outs, scratch, *operands, far=()):
    vmem = pl.BlockSpec(memory_space=pltpu.VMEM)
    in_specs = [pl.BlockSpec(memory_space=pl.ANY) if i in far else vmem for i in range(len(operands))]
    return pl.pallas_call(
        kernel,
        out_shape=[jax.ShapeDtypeStruct(shape, kind) for shape, kind in outs],
        in_specs=in_specs,
        out_specs=[vmem] * len(outs),
        scratch_shapes=scratch,
        compiler_params=pltpu.CompilerParams(
            collective_id=collective_id, has_side_effects=True, vmem_limit_bytes=56 * 2**20
        ),
    )(*operands)


def dma_sems(*counts):
    return [pltpu.SemaphoreType.DMA((count,)) for count in counts]


def sum_scratch(rows):
    return [pltpu.VMEM((4, rows, D), LOW) for _ in range(3)]


def matmul(left_in, right_in):
    return jnp.dot(left_in, right_in, preferred_element_type=F32)


def outer_product(left_in, right_in):
    return jnp.einsum("tc,td->cd", left_in, right_in, preferred_element_type=F32)


def back_product(grad_in, weight_in):
    return jnp.einsum("tc,dc->td", grad_in, weight_in, preferred_element_type=F32)


def rope_angles(token_pos, head_width):
    half_width = head_width // 2
    freq_index = jnp.arange(half_width, dtype=F32)
    inverse_freq = jnp.exp(freq_index * (-2.0 * math.log(rope_base) / head_width))
    angles = token_pos.astype(F32)[:, None] * inverse_freq[None, :]
    return (jnp.cos(angles), jnp.sin(angles))


def rotate(values, cosine, sine_vals):
    half_width = values.shape[-1] // 2
    first_half = values[:, :half_width]
    second_half = values[:, half_width:]
    return jnp.concatenate(
        [
            first_half * cosine - second_half * sine_vals,
            second_half * cosine + first_half * sine_vals,
        ],
        axis=-1,
    )


def silu_slope(pre_act):
    sigmoid_gate = jax.nn.sigmoid(pre_act)
    return sigmoid_gate * (1.0 + pre_act * (1.0 - sigmoid_gate))


def attend_forward(query_in, key_in, value_in, allowed, score_scale):
    scores = back_product(query_in, key_in) * score_scale
    scores = jnp.where(allowed, scores, masked_score)
    row_peak = jnp.max(scores, axis=1, keepdims=True)
    logsum = row_peak + jnp.log(jnp.sum(jnp.exp(scores - row_peak), axis=1, keepdims=True))
    softmax_low = jnp.exp(scores - logsum).astype(LOW)
    return matmul(softmax_low, value_in).astype(LOW), logsum


def attend_backward(query_in, key_in, value_in, allowed, score_scale, result, logsum, grad_result):
    row_delta = jnp.sum(grad_result.astype(F32) * result.astype(F32), axis=1, keepdims=True)
    scores = back_product(query_in, key_in) * score_scale
    scores = jnp.where(allowed, scores, masked_score)
    softmax_f = jnp.exp(scores - logsum)
    grad_value = outer_product(softmax_f.astype(LOW), grad_result)
    grad_probs = back_product(grad_result, value_in)
    grad_scores = (softmax_f * (grad_probs - row_delta)).astype(LOW)
    grad_query = matmul(grad_scores, key_in) * score_scale
    grad_key = outer_product(grad_scores, query_in) * score_scale
    return (grad_query, grad_key, grad_value)


def mamba_core(mixed_in, step_raw, conv_taps, log_rate, bias_step, skip_gain, segment_ids, allowed):
    total_rows, col_width = mixed_in.shape
    head_count = step_raw.shape[1]
    conv_sum = conv_taps[0][None, :] * mixed_in
    for shift_lag in range(1, conv_taps.shape[0]):
        shifted = jnp.concatenate(
            [jnp.zeros((shift_lag, col_width), mixed_in.dtype), mixed_in[:-shift_lag]], axis=0
        )
        same_seq = jnp.concatenate(
            [
                jnp.zeros((shift_lag,), dtype=bool),
                segment_ids[shift_lag:] == segment_ids[:-shift_lag],
            ],
            axis=0,
        )
        conv_sum = conv_sum + conv_taps[shift_lag][None, :] * jnp.where(
            same_seq[:, None], shifted, 0.0
        )
    activated = jax.nn.silu(conv_sum)
    head_in = activated[:, : head_count * MP].reshape(total_rows, head_count, MP)
    state_in = activated[:, head_count * MP : head_count * MP + NS]
    state_out = activated[:, head_count * MP + NS :]
    step_size = jax.nn.softplus(step_raw + bias_step[None, :])
    log_rates = -step_size * jnp.exp(log_rate)[None, :]
    order = jnp.arange(total_rows, dtype=jnp.int32)
    before = (order[:, None] >= order[None, :]).astype(F32)
    cumulative = jnp.einsum("sh,ts->ht", log_rates, before, precision=highest)
    intersection = jnp.dot(state_out, state_in.T, precision=highest)
    log_gap = cumulative[:, :, None] - cumulative[:, None, :]
    decay_mat = jnp.exp(jnp.where(allowed[None, :, :], log_gap, masked_score))
    mixing = intersection[None, :, :] * decay_mat * step_size.T[:, None, :]
    result = (
        jnp.einsum("hts,shp->thp", mixing, head_in, precision=highest)
        + skip_gain[None, :, None] * head_in
    )
    return result.reshape(total_rows, head_count * MP)


def body(
    hidden_in,
    cotangent,
    segment_ids,
    positions,
    w_query,
    w_key,
    w_value,
    w_mamba_gate,
    w_mamba_in,
    w_mamba_bcdt,
    w_attention_out,
    w_mamba_out,
    w_feed_gate,
    w_feed_up,
    w_feed_down,
    gain_mixer,
    gain_feed,
    conv_weight,
    log_decay,
    step_bias,
    skip_scale,
):
    s, t, d = lax.axis_index("seq"), lax.axis_index("tensor"), lax.axis_index("dp")
    seq_count, tensor_count, dp_count = (
        lax.axis_size("seq"),
        lax.axis_size("tensor"),
        lax.axis_size("dp"),
    )
    length = segment_ids.shape[0]
    rows = hidden_in.shape[0] // tensor_count
    owner = w_query.shape[0]
    heads_dev = MH // (seq_count * tensor_count)
    width = heads_dev * MP
    group = t * seq_count + s
    score_scale = HD ** (-0.5)
    feed_width = w_feed_gate.shape[1] // seq_count

    def own(weight, size, dim):
        return lax.dynamic_slice_in_dim(weight, s * size, size, dim)

    aux = lax.select_n(
        s, w_key, w_value, w_mamba_bcdt[:, :NS], w_mamba_bcdt[:, NS : 2 * NS]
    )
    entry_own = jnp.concatenate(
        [own(w_query, HD, 1), aux, own(w_mamba_gate, width, 1), own(w_mamba_in, width, 1)], axis=1
    )
    outs_own = jnp.concatenate(
        [own(w_attention_out, HD, 0), own(w_mamba_out, width, 0), own(w_feed_down, feed_width, 0)],
        axis=0,
    ).T
    feed_own = jnp.concatenate([own(w_feed_gate, feed_width, 1), own(w_feed_up, feed_width, 1)], axis=1)
    step_cols = lax.dynamic_slice_in_dim(w_mamba_bcdt, 2 * NS + group * heads_dev, heads_dev, 1)
    spare = jnp.concatenate(
        [step_cols.T.astype(F32), gain_mixer[None].astype(F32), gain_feed[None].astype(F32)], axis=0
    )
    spare = lax.dynamic_update_slice(jnp.zeros((8, D), F32), spare, (0, d * owner))
    my_rows = lambda array: lax.dynamic_slice_in_dim(array, t * rows, rows, 0)
    hid_own, cot_own = my_rows(hidden_in), my_rows(cotangent)
    cosine, sine_vals = rope_angles(positions, HD)
    cos_table = jnp.concatenate([cosine, cosine], axis=1)
    sin_table = jnp.concatenate([-sine_vals, sine_vals], axis=1)
    row_meta = jnp.zeros((8, length), F32).at[:2].set(
        jnp.stack([segment_ids, positions]).astype(F32)
    )
    col_meta = row_meta.T
    conv_taps = jnp.concatenate(
        [conv_weight[:, MD:], lax.dynamic_slice_in_dim(conv_weight, group * width, width, 1)], axis=1
    )
    per_head = lambda vector: lax.dynamic_slice_in_dim(vector, group * heads_dev, heads_dev, 0)
    head_meta = jnp.zeros((8, 128), F32).at[:heads_dev, :3].set(
        jnp.stack([per_head(step_bias), per_head(log_decay), per_head(skip_scale)], axis=1)
    )
    n = dp_count
    (
        spare_full, tokens, entry_w, feed_w, outs_w, kv, query_low, gate_pre, x_low, step_rows, mixed, ssm_low,
        logsum, middle_own, feed_in,
    ) = call(
        functools.partial(forward_kernel, dp_count, heads_dev),
        1,
        [
            ((8, D), F32),
            ((length, 2 * D), LOW),
            ((D, entry_own.shape[1]), LOW),
            ((D, feed_own.shape[1]), LOW),
            ((D, outs_own.shape[1]), LOW),
            ((seq_count, length, HD), LOW),
            ((length, HD), LOW),
            ((length, width), F32),
            ((length, width), LOW),
            ((8, length), F32),
            ((length, HD + width), LOW),
            ((length, width), LOW),
            ((length, 1), F32),
            ((rows, D), F32),
            ((length, D), LOW),
        ],
        [
            pltpu.VMEM((n, 8, D), F32),
            pltpu.VMEM((seq_count, tensor_count, rows, D), LOW),
            *sum_scratch(rows),
            pltpu.SemaphoreType.DMA((8, n)),
            *dma_sems(3, 7, 7, 8, 8, 7, 7, 4, 4),
        ],
        spare, hid_own, cot_own, entry_own, feed_own, outs_own, cos_table, sin_table, col_meta, row_meta, conv_taps, head_meta,
        far=(3, 4, 5),
    )
    mixer_in, cot_low = tokens[:, :D], tokens[:, D:]
    step_w = spare_full[:heads_dev].astype(LOW)
    gate_end, in_end = 2 * HD + width, 2 * HD + 2 * width
    out_w, down_w = outs_w[:, : HD + width], outs_w[:, HD + width :]
    parts_shape = (seq_count, tensor_count, rows, D)
    key_low, value_low, state_in, state_out = kv[0], kv[1], kv[2], kv[3]
    attended = mixed[:, :HD]
    allowed = (segment_ids[:, None] == segment_ids[None, :]) & (
        positions[None, :] <= positions[:, None]
    )
    core = functools.partial(mamba_core, segment_ids=segment_ids, allowed=allowed)
    _, pullback = jax.vjp(
        core,
        jnp.concatenate([x_low, state_in, state_out], axis=1).astype(F32),
        step_rows[:heads_dev].T,
        jnp.concatenate([conv_taps[:, 2 * NS :], conv_taps[:, : 2 * NS]], axis=1),
        per_head(log_decay),
        per_head(step_bias),
        per_head(skip_scale),
    )
    silu_gate = jax.nn.silu(gate_pre)
    feed_pre = matmul(feed_in, feed_w)
    feed_gate, feed_up = feed_pre[:, :feed_width], feed_pre[:, feed_width:]
    activated = (jax.nn.silu(feed_gate) * feed_up).astype(LOW)
    grad_act = matmul(cot_low, down_w)
    grad_feed_both = jnp.concatenate(
        [grad_act * feed_up * silu_slope(feed_gate), grad_act * jax.nn.silu(feed_gate)], axis=1
    ).astype(LOW)
    feed_part = back_product(grad_feed_both, feed_w).astype(LOW).reshape(parts_shape)
    grad_own, gain_feed_part, middle_low = call(
        feed_back_kernel,
        3,
        [((rows, D), F32), ((8, D), F32), ((length, D), LOW)],
        [*sum_scratch(rows), *dma_sems(8, 8, 7, 7)],
        feed_part,
        middle_own,
        spare_full,
        cot_own,
    )
    output_part = back_product(activated, down_w).astype(LOW).reshape(parts_shape)
    grad_feed_w = ring_scatter(outer_product(feed_in, grad_feed_both), "dp", 0)
    grad_down_w = ring_scatter(outer_product(cot_low, activated), "dp", 0)

    grad_out = matmul(middle_low, out_w)
    grad_out_w = ring_scatter(outer_product(middle_low, mixed), "dp", 0)
    grad_gated = grad_out[:, HD:]
    grad_attended = grad_out[:, :HD].astype(LOW)
    grad_ssm = (grad_gated * silu_gate).astype(LOW)
    grad_gate_in = (grad_gated * ssm_low.astype(F32) * silu_slope(gate_pre)).astype(LOW)
    grad_query, grad_key, grad_value = attend_backward(
        query_low, key_low, value_low, allowed, score_scale, attended, logsum, grad_attended
    )
    dq_low = rotate(grad_query, cosine, -sine_vals).astype(LOW)
    dk_low = rotate(grad_key, cosine, -sine_vals).astype(LOW)
    core_grads = pullback(grad_ssm.astype(F32))
    dx_low = core_grads[0][:, :width].astype(LOW)
    dstate = core_grads[0][:, width:].astype(LOW)
    dstep_low = core_grads[1].astype(LOW)
    aux_stack = jnp.stack([dk_low, grad_value.astype(LOW), dstate[:, :NS], dstate[:, NS:]])
    aux_own = lax.dynamic_index_in_dim(aux_stack, s, 0, keepdims=False).astype(F32)
    for k in (1, 2, 3):
        theirs = lax.dynamic_index_in_dim(aux_stack, s ^ k, 0, keepdims=False)
        aux_own = aux_own + lax.ppermute(theirs, "seq", [(i, i ^ k) for i in range(4)]).astype(F32)
    from_other = lax.ppermute(aux_own.astype(LOW), "tensor", [(0, 1), (1, 0)]).astype(F32)
    daux_low = (aux_own + jnp.where(s >= 2, from_other, 0.0)).astype(LOW)
    once = (s < 2) | (t == 0)
    back_own = jnp.concatenate([dq_low, daux_low, grad_gate_in, dx_low], axis=1)
    back_once = jnp.concatenate(
        [dq_low, jnp.where(once, daux_low, jnp.zeros_like(daux_low)), grad_gate_in, dx_low], axis=1
    )
    input_part = (back_product(back_once, entry_w) + matmul(dstep_low, step_w)).astype(LOW)
    grad_entry_w = ring_scatter(outer_product(mixer_in, back_own), "dp", 0)
    out_two, hid_two, gain_mixer_part = call(
        last_kernel,
        4,
        [((2, rows, D), F32), ((2, rows, D), F32), ((8, D), F32)],
        [*sum_scratch(rows), *sum_scratch(rows), *dma_sems(8, 8, 8, 8, 2, 2)],
        output_part,
        input_part.reshape(parts_shape),
        middle_own,
        hid_own,
        spare_full,
        grad_own,
    )
    output, grad_hidden = out_two.reshape(2 * rows, D), hid_two.reshape(2 * rows, D)

    conv_size, state_size = KCONV * width, KCONV * 2 * NS
    lanes = jnp.concatenate(
        [
            gain_mixer_part[0],
            gain_feed_part[0],
            outer_product(dstep_low, mixer_in).reshape(-1),
            core_grads[2][:, :width].reshape(conv_size),
            core_grads[2][:, width:].reshape(state_size),
            core_grads[3],
            core_grads[4],
            core_grads[5],
        ]
    )
    small_rows = -(-lanes.shape[0] // 1024) * 8
    lanes = jnp.pad(lanes, (0, small_rows * 128 - lanes.shape[0])).reshape(small_rows, 128)
    (small_all,) = call(
        functools.partial(small_kernel, dp_count),
        5,
        [((8, small_rows, 128), F32)],
        [pltpu.VMEM((dp_count, small_rows, 128), F32), *dma_sems(dp_count, dp_count, 7, 7)],
        lanes,
    )
    small_all = small_all.reshape(seq_count, tensor_count, -1)
    by_row = small_all[..., : (2 + heads_dev) * D].reshape(seq_count, tensor_count, 2 + heads_dev, D)
    by_row = lax.dynamic_slice_in_dim(by_row, d * owner, owner, 3)
    owned_gain = jnp.sum(by_row[:, :, :2], axis=(0, 1))
    grad_step_w = by_row[:, :, 2:].transpose(1, 0, 2, 3).reshape(MH, owner).T
    conv_start = (2 + heads_dev) * D
    conv_x = small_all[..., conv_start : conv_start + conv_size]
    conv_x = conv_x.reshape(seq_count, tensor_count, KCONV, width).transpose(2, 1, 0, 3)
    state_start = conv_start + conv_size
    conv_state = jnp.sum(small_all[..., state_start : state_start + state_size], axis=(0, 1))
    grad_conv_weight = jnp.concatenate(
        [conv_x.reshape(KCONV, MD), conv_state.reshape(KCONV, 2 * NS)], axis=1
    )
    head_start = state_start + state_size
    heads = small_all[..., head_start : head_start + 3 * heads_dev]
    heads = heads.reshape(seq_count, tensor_count, 3, heads_dev).transpose(2, 1, 0, 3).reshape(3, MH)

    feed_blocks = [b.astype(F32) for b in ring_gather(grad_feed_w.astype(LOW), "seq")]
    down_blocks = [b.astype(F32) for b in ring_gather(grad_down_w.astype(LOW), "seq")]
    out_blocks = [b.astype(F32) for b in ring_gather(grad_out_w.astype(LOW), "seq")]
    entry_blocks = [b.astype(F32) for b in ring_gather(grad_entry_w.astype(LOW), "seq")]
    side = lambda blocks, low, high: jnp.concatenate([b[:, low:high] for b in blocks], axis=1)
    below = lambda blocks, low, high: jnp.concatenate([b[:, low:high].T for b in blocks], axis=0)
    return (
        output,
        grad_hidden,
        side(entry_blocks, 0, HD),
        entry_blocks[0][:, HD : 2 * HD],
        entry_blocks[1][:, HD : 2 * HD],
        side(entry_blocks, 2 * HD, gate_end),
        side(entry_blocks, gate_end, in_end),
        jnp.concatenate([entry_blocks[2][:, HD : 2 * HD], entry_blocks[3][:, HD : 2 * HD], grad_step_w], axis=1),
        below(out_blocks, 0, HD),
        below(out_blocks, HD, HD + width),
        side(feed_blocks, 0, feed_width),
        side(feed_blocks, feed_width, 2 * feed_width),
        below(down_blocks, 0, feed_width),
        owned_gain[0],
        owned_gain[1],
        grad_conv_weight,
        heads[0],
        heads[1],
        heads[2],
    )


def solution(mesh):
    return jax.shard_map(
        body,
        mesh=mesh,
        in_specs=(
            P(("dp", "seq"), None),
            P(("dp", "seq"), None),
            P("dp"),
            P("dp"),
            P("dp", "tensor"),
            P("dp", "tensor"),
            P("dp", "tensor"),
            P("dp", "tensor"),
            P("dp", "tensor"),
            P("dp", None),
            P("tensor", "dp"),
            P("tensor", "dp"),
            P("dp", "tensor"),
            P("dp", "tensor"),
            P("tensor", "dp"),
            P("dp"),
            P("dp"),
            P(),
            P(),
            P(),
            P(),
        ),
        out_specs=(
            P(("dp", "seq"), None),
            P(("dp", "seq"), None),
            P("dp", "tensor"),
            P("dp", "tensor"),
            P("dp", "tensor"),
            P("dp", "tensor"),
            P("dp", "tensor"),
            P("dp", None),
            P("tensor", "dp"),
            P("tensor", "dp"),
            P("dp", "tensor"),
            P("dp", "tensor"),
            P("tensor", "dp"),
            P("dp"),
            P("dp"),
            P(),
            P(),
            P(),
            P(),
        ),
        check_vma=False,
    )
```

```python
import functools
import math

import jax
import jax.numpy as jnp
from jax import lax
from jax.experimental import pallas as pl
from jax.experimental.pallas import tpu as pltpu
from jax.sharding import PartitionSpec as P

D = 1024
HD = 128
MH = 24
MP = 64
NS = 128
KCONV = 4
MD = 1536

MESH = pl.DeviceIdType.MESH
LOW = jnp.bfloat16
F32 = jnp.float32

epsilon = 1e-05
rope_base = 100000000000.0
masked_score = -1e30
highest = lax.Precision.HIGHEST


def seq_partner(seq_index, k):
    if k == 1:
        return seq_index + 1 - 2 * (seq_index % 2)
    if k == 2:
        return seq_index + 2 - 4 * (seq_index // 2)
    return 3 - seq_index


def greet(devices):
    barrier = pltpu.get_barrier_semaphore()
    for device in devices:
        pl.semaphore_signal(barrier, inc=1, device_id=device, device_id_type=MESH)
    pl.semaphore_wait(barrier, len(devices))


def plane_peers():
    s, t = lax.axis_index("seq"), lax.axis_index("tensor")
    return [{"seq": seq_partner(s, k), "tensor": t} for k in (1, 2, 3)] + [
        {"seq": s, "tensor": 1 - t}
    ]


def send(src, dst, send_sem, recv_sem, device):
    copy = pltpu.make_async_remote_copy(
        src_ref=src,
        dst_ref=dst,
        send_sem=send_sem,
        recv_sem=recv_sem,
        device_id=device,
        device_id_type=MESH,
    )
    copy.start()
    return copy


def spread_begin(out_ref, rows, sems):
    s, t = lax.axis_index("seq"), lax.axis_index("tensor")
    mine = out_ref.at[pl.ds(pl.multiple_of((2 * s + t) * rows, rows), rows)]
    devices = [{"seq": s, "tensor": 1 - t}] + [{"seq": seq_partner(s, k), "tensor": t} for k in (1, 2, 3)]
    return [send(mine, mine, sems.at[0, k], sems.at[1, k], devices[k]) for k in (1, 2, 3, 0)]


def spread_end(out_ref, rows, sems, copies):
    s, t = lax.axis_index("seq"), lax.axis_index("tensor")
    for k in (1, 2, 3):
        copies[k - 1].wait_recv()
        came = out_ref.at[pl.ds(pl.multiple_of((2 * seq_partner(s, k) + t) * rows, rows), rows)]
        copies.append(send(came, came, sems.at[0, 3 + k], sems.at[1, 3 + k], {"seq": s, "tensor": 1 - t}))
    for copy in copies[3:]:
        copy.wait_recv()
    for copy in copies:
        copy.wait_send()


def plane_order():
    s = lax.axis_index("seq")
    return [s, seq_partner(s, 1), seq_partner(s, 2), seq_partner(s, 3)]


def sum_begin(part_ref, near_ref, sems):
    s, t = lax.axis_index("seq"), lax.axis_index("tensor")
    to = plane_order()
    return {
        k: send(part_ref.at[to[k], 1 - t], near_ref.at[k], sems.at[0, k], sems.at[1, k], {"seq": s, "tensor": 1 - t})
        for k in (3, 1, 2, 0)
    }


def sum_middle(part_ref, near_ref, low_ref, far_ref, sems, near):
    t = lax.axis_index("tensor")
    to, far = plane_order(), {}
    for k in (3, 1, 2):
        near[k].wait_recv()
        low_ref[k] = (part_ref[to[k], t].astype(F32) + near_ref[k].astype(F32)).astype(LOW)
        far[k] = send(
            low_ref.at[k], far_ref.at[k], sems.at[0, 4 + k], sems.at[1, 4 + k], {"seq": to[k], "tensor": t}
        )
    return far


def sum_end(part_ref, near_ref, far_ref, near, far):
    s, t = lax.axis_index("seq"), lax.axis_index("tensor")
    near[0].wait_recv()
    total = part_ref[s, t].astype(F32) + near_ref[0].astype(F32)
    for k in (1, 2, 3):
        far[k].wait_recv()
        total = total + far_ref[k].astype(F32)
    for copy in (*near.values(), *far.values()):
        copy.wait_send()
    return total


def dot_nt(left, right, precision=None):
    return lax.dot_general(left, right, (((1,), (1,)), ((), ())), precision=precision, preferred_element_type=F32)


def dot_tn(left, right, precision=None):
    return lax.dot_general(left, right, (((0,), (0,)), ((), ())), precision=precision, preferred_element_type=F32)


def dot_nn(left, right, precision=None):
    return lax.dot_general(left, right, (((1,), (0,)), ((), ())), precision=precision, preferred_element_type=F32)


def turn(values, cos_ref, sin_ref):
    return values * cos_ref[...] + pltpu.roll(values, HD // 2, 1) * sin_ref[...]


def turn_back(values, cos_ref, sin_ref):
    return values * cos_ref[...] - pltpu.roll(values, HD // 2, 1) * sin_ref[...]


def visible(col_ref, row_ref):
    return (col_ref[:, 0:1] == row_ref[0:1, :]) & (row_ref[1:2, :] <= col_ref[:, 1:2])


def convolve(mixed, taps_ref, col_ref):
    total = taps_ref[0:1] * mixed
    for lag in range(1, KCONV):
        kept = jnp.where(col_ref[:, 1:2] >= lag, pltpu.roll(mixed, lag, 0), 0.0)
        total = total + taps_ref[lag : lag + 1] * kept
    return total


def steps_and_sums(raw, head_ref, heads, summed=True):
    raw = jnp.where(lax.broadcasted_iota(jnp.int32, raw.shape, 0) < heads, raw, 0.0)
    pre = raw + head_ref[:, 0:1]
    step = jnp.maximum(pre, 0.0) + jnp.log1p(jnp.exp(-jnp.abs(pre)))
    rate = -step * jnp.exp(head_ref[:, 1:2])
    if not summed:
        return pre, step, rate, None
    length = raw.shape[1]
    upto = lax.broadcasted_iota(jnp.int32, (length, length), 0) <= lax.broadcasted_iota(
        jnp.int32, (length, length), 1
    )
    return pre, step, rate, dot_nn(rate, upto.astype(F32), highest)


def dp_sends(dp_count, src_of, dst_of, sems, row):
    d = lax.axis_index("dp")
    return [
        send(
            src_of(lax.rem(d + k, dp_count)), dst_of(k), sems.at[row, k], sems.at[row + 1, k],
            {"dp": lax.rem(d + k, dp_count)},
        )
        for k in range(1, dp_count)
    ]


def convolve_back(grad, mixed, taps_ref, col_ref):
    length = grad.shape[0]
    total = taps_ref[0:1] * grad
    taps = [jnp.sum(grad * mixed, axis=0, keepdims=True)]
    for lag in range(1, KCONV):
        kept = jnp.where(col_ref[:, 1:2] >= lag, grad, 0.0)
        total = total + taps_ref[lag : lag + 1] * pltpu.roll(kept, length - lag, 0)
        taps.append(jnp.sum(kept * pltpu.roll(mixed, lag, 0), axis=0, keepdims=True))
    return total, jnp.concatenate(taps, axis=0)


def norm_backward(grad, values, gain, upstream):
    scale = lax.rsqrt(jnp.mean(values * values, axis=1, keepdims=True) + epsilon)
    normed = values * scale
    grad_gain = jnp.sum(grad * normed, axis=0, keepdims=True)
    inner = grad * gain
    result = upstream + scale * (inner - normed * jnp.mean(inner * normed, axis=1, keepdims=True))
    return result, grad_gain


def silu_slope(pre_act):
    sigmoid_gate = jax.nn.sigmoid(pre_act)
    return sigmoid_gate * (1.0 + pre_act * (1.0 - sigmoid_gate))


def rounded_part(part_ref, value):
    part_ref[...] = value.astype(LOW).reshape(part_ref.shape)


def layer_kernel(
    dp_count, heads,
    spare_ref, hid_ref, cot_ref, entry_own, feed_own, outs_own, cos_ref, sin_ref, col_ref, row_ref, taps_ref, head_ref,
    out_ref, hid_grad_ref, fin_feed, fin_outs, fin_entry, fin_aux, small_all, gain_all,
    came, tok_ref, feed_ref, low_ref, entry_w, feed_w, outs_w, kv_ref, query_ref, gate_ref, x_ref, step_ref, mixed_ref,
    ssm_ref, prob_ref, decay_ref, meet_ref, middle_ref, grad_ref, dboth_ref, act_ref, back_ref,
    part, near, low, far, gs_feed, gs_outs, gs_entry, gs_aux, gr_feed, gr_outs, gr_entry, gr_aux,
    aux_send, aux_recv, aux_near, small, small_came, gain, gain_came,
    dp_sem, local, plane_sem, fin_sem, kv_sem, aux_sem, small_sem, gain_sem,
):
    d, s, t = lax.axis_index("dp"), lax.axis_index("seq"), lax.axis_index("tensor")
    rows, owner, width = hid_ref.shape[0], entry_own.shape[0], heads * MP
    length = tok_ref.shape[0]
    other = {"seq": s, "tensor": 1 - t}
    peers = []
    for k in range(4):
        for flip in range(2):
            if k or flip:
                peers.append({"seq": s if k == 0 else seq_partner(s, k), "tensor": 1 - t if flip else t})
    seq_peers = [{"seq": seq_partner(s, k), "tensor": t} for k in (1, 2, 3)]
    greet(peers + [{"dp": lax.rem(d + k, dp_count)} for k in range(1, dp_count)])
    to_send = []
    place = pl.ds(pl.multiple_of(d * owner, owner), owner)
    spares = dp_sends(dp_count, lambda j: spare_ref, lambda k: came.at[k], dp_sem, 0)
    entries = dp_sends(dp_count, lambda j: entry_own, lambda k: entry_w.at[place], dp_sem, 2)
    locals_ = [
        pltpu.make_async_copy(own, full.at[place], local.at[i])
        for i, (own, full) in enumerate(((entry_own, entry_w), (feed_own, feed_w), (outs_own, outs_w)))
    ]
    for copy in locals_:
        copy.start()
    hid = hid_ref[...]
    normed = hid * lax.rsqrt(jnp.mean(hid * hid, axis=1, keepdims=True) + epsilon)
    total = spare_ref[...]
    for k in range(1, dp_count):
        spares[k - 1].wait_recv()
        total = total + came[k]
    gain_one, gain_two, step_w = total[3:4], total[4:5], total.astype(LOW)
    mine = pl.ds(pl.multiple_of((2 * s + t) * rows, rows), rows)
    tok_ref[mine, :D] = (normed * gain_one).astype(LOW)
    tok_ref[mine, D:] = cot_ref[...].astype(LOW)
    spread_end(tok_ref, rows, plane_sem.at[0], spread_begin(tok_ref, rows, plane_sem.at[0]))
    for copy in entries:
        copy.wait_recv()
    outers = dp_sends(dp_count, lambda j: outs_own, lambda k: outs_w.at[place], dp_sem, 4)
    feeds = dp_sends(dp_count, lambda j: feed_own, lambda k: feed_w.at[place], dp_sem, 6)
    for copy in locals_:
        copy.wait()

    mixer_in = tok_ref[:, :D]
    aux = dot_nn(mixer_in, entry_w[:, HD : 2 * HD])
    is_key = jnp.where(s == 0, 1.0, 0.0)
    aux = turn(aux, cos_ref, sin_ref) * is_key + aux * (1.0 - is_key)
    kv_ref[s] = aux.astype(LOW)
    shared = [
        send(kv_ref.at[s], kv_ref.at[s], kv_sem.at[0, i], kv_sem.at[1, i], peer)
        for i, peer in enumerate(seq_peers)
    ]
    query_ref[...] = turn(dot_nn(mixer_in, entry_w[:, :HD]), cos_ref, sin_ref).astype(LOW)
    gate_x = dot_nn(mixer_in, entry_w[:, 2 * HD :])
    gate_ref[...] = gate_x[:, :width]
    x_ref[...] = gate_x[:, width:].astype(LOW)
    step_ref[...] = dot_nt(step_w, mixer_in).astype(LOW).astype(F32)
    _, step, _, cum = steps_and_sums(step_ref[...], head_ref, heads)
    columns = jnp.concatenate([cum, step], axis=0).T
    cum_col, step_col = columns[:, :8], columns[:, 8:]
    x_conv = convolve(x_ref[...].astype(F32), taps_ref.at[:, 2 * NS :], col_ref)
    x_act = x_conv * jax.nn.sigmoid(x_conv)
    allowed = visible(col_ref, row_ref)
    for copy in shared:
        copy.wait_recv()

    scores = jnp.where(allowed, dot_nt(query_ref[...], kv_ref[0]) * HD ** (-0.5), masked_score)
    peak = jnp.max(scores, axis=1, keepdims=True)
    logsum = peak + jnp.log(jnp.sum(jnp.exp(scores - peak), axis=1, keepdims=True))
    probs = jnp.exp(scores - logsum)
    prob_ref[...] = probs
    mixed_ref[:, :HD] = dot_nn(probs.astype(LOW), kv_ref[1]).astype(LOW)

    def state(index):
        conv = convolve(kv_ref[2 + index].astype(F32), taps_ref.at[:, index * NS : (index + 1) * NS], col_ref)
        return conv

    bconv, cconv = state(0), state(1)
    bstate, cstate = bconv * jax.nn.sigmoid(bconv), cconv * jax.nn.sigmoid(cconv)
    meet_ref[...] = dot_nt(cstate, bstate, highest)
    sums = []
    for h in range(heads):
        decay = jnp.exp(jnp.where(allowed, cum_col[:, h : h + 1] - cum[h : h + 1, :], masked_score))
        decay_ref[h] = decay
        x_head = x_act[:, h * MP : (h + 1) * MP]
        sums.append(dot_nn(meet_ref[...] * decay, x_head * step_col[:, h : h + 1], highest))
    core_out = jnp.concatenate(sums, axis=1)
    skips = jnp.concatenate(
        [jnp.broadcast_to(head_ref[h : h + 1, 2:3], (1, MP)) for h in range(heads)], axis=1
    )
    ssm_ref[...] = core_out
    ssm_low = (core_out + skips * x_act).astype(LOW).astype(F32)
    gate_pre = gate_ref[...]
    mixed_ref[:, HD:] = (ssm_low * (gate_pre * jax.nn.sigmoid(gate_pre))).astype(LOW)

    for copy in outers:
        copy.wait_recv()
    down_start = HD + act_ref.shape[1]
    rounded_part(
        part.at[0],
        dot_nt(mixed_ref[:, :HD], outs_w[:, :HD]) + dot_nt(mixed_ref[:, HD:], outs_w[:, down_start:]),
    )

    def begin(i):
        return sum_begin(part.at[i], near.at[i], plane_sem.at[1 + i])

    def middle_of(i, copies):
        return sum_middle(part.at[i], near.at[i], low.at[i], far.at[i], plane_sem.at[1 + i], copies)

    def end(i, copies, later):
        return sum_end(part.at[i], near.at[i], far.at[i], copies, later)

    sum_near = begin(0)
    middle = hid_ref[...] + end(0, sum_near, middle_of(0, sum_near))
    middle_ref[...] = middle
    scale = lax.rsqrt(jnp.mean(middle * middle, axis=1, keepdims=True) + epsilon)
    feed_ref[mine, :] = (middle * scale * gain_two).astype(LOW)
    spread_end(feed_ref, rows, plane_sem.at[5], spread_begin(feed_ref, rows, plane_sem.at[5]))
    for copy in feeds:
        copy.wait_recv()

    half = act_ref.shape[1]
    feed_gate = dot_nn(feed_ref[...], feed_w[:, :half])
    feed_up = dot_nn(feed_ref[...], feed_w[:, half:])
    feed_sig = jax.nn.sigmoid(feed_gate)
    feed_silu = feed_gate * feed_sig
    act_ref[...] = (feed_silu * feed_up).astype(LOW)
    grad_act = dot_nn(tok_ref[:, D:], outs_w[:, HD:down_start])
    dboth_ref[:, :half] = (grad_act * feed_up * (feed_sig * (1.0 + feed_gate * (1.0 - feed_sig)))).astype(LOW)
    dboth_ref[:, half:] = (grad_act * feed_silu).astype(LOW)
    rounded_part(part.at[1], dot_nt(dboth_ref[...], feed_w[...]))
    sum_near = begin(1)
    gs_feed[:, : 2 * half] = dot_tn(feed_ref[...], dboth_ref[...]).astype(LOW)
    sum_far = middle_of(1, sum_near)
    gs_feed[:, 2 * half :] = dot_tn(tok_ref[:, D:], act_ref[...]).astype(LOW)

    def reduce_begin(gs, gr, row):
        return dp_sends(
            dp_count,
            lambda j: gs.at[pl.ds(pl.multiple_of(j * owner, owner), owner)],
            lambda k: gr.at[k],
            dp_sem,
            row,
        )

    def reduce_end(gs, gr, fin, copies, row):
        value = gs[place].astype(F32)
        for k in range(1, dp_count):
            copies[k - 1].wait_recv()
            value = value + gr[k].astype(F32)
        fin[s] = value.astype(LOW)
        return [
            send(fin.at[s], fin.at[s], fin_sem.at[row, 0, i], fin_sem.at[row, 1, i], peer)
            for i, peer in enumerate(seq_peers)
        ]

    feed_red = reduce_begin(gs_feed, gr_feed, 8)
    grad_middle, grad_gain_two = norm_backward(end(1, sum_near, sum_far), middle_ref[...], gain_two, cot_ref[...])
    grad_ref[...] = grad_middle
    low_ref[mine, :] = grad_middle.astype(LOW)
    spread = spread_begin(low_ref, rows, plane_sem.at[6])
    rounded_part(part.at[2], dot_nt(act_ref[...], outs_w[:, HD:down_start]))
    spread_end(low_ref, rows, plane_sem.at[6], spread)
    out_near = begin(2)

    grad_gated = dot_nn(low_ref[...], outs_w[:, down_start:])
    grad_attended = dot_nn(low_ref[...], outs_w[:, :HD]).astype(LOW)
    gs_outs[...] = dot_tn(low_ref[...], mixed_ref[...]).astype(LOW)
    outs_red = reduce_begin(gs_outs, gr_outs, 10)
    gate_sig = jax.nn.sigmoid(gate_pre)
    back_ref[:, HD : HD + width] = (
        grad_gated * ssm_low * (gate_sig * (1.0 + gate_pre * (1.0 - gate_sig)))
    ).astype(LOW)
    dy = (grad_gated * (gate_pre * gate_sig)).astype(LOW).astype(F32)

    row_delta = jnp.sum(grad_attended.astype(F32) * mixed_ref[:, :HD].astype(F32), axis=1, keepdims=True)
    probs = prob_ref[...]
    aux_send[1] = dot_tn(probs.astype(LOW), grad_attended).astype(LOW)
    dscores = (probs * (dot_nt(grad_attended, kv_ref[1]) - row_delta)).astype(LOW)
    back_ref[:, :HD] = turn_back(dot_nn(dscores, kv_ref[0]) * HD ** (-0.5), cos_ref, sin_ref).astype(LOW)
    aux_send[0] = turn_back(dot_tn(dscores, query_ref[...]) * HD ** (-0.5), cos_ref, sin_ref).astype(LOW)
    out_far = middle_of(2, out_near)

    dmeet = jnp.zeros((length, length), F32)
    dx_parts, dcum_cols, dstep_cols, dskips = [], [], [], []
    for h in range(heads):
        cols = slice(h * MP, (h + 1) * MP)
        step_h = step_col[:, h : h + 1]
        dy_h, x_h = dy[:, cols], x_act[:, cols]
        u_h = x_h * step_h
        du = dot_tn(meet_ref[...] * decay_ref[h], dy_h, highest)
        dmeet = dmeet + dot_nt(dy_h, u_h, highest) * decay_ref[h]
        dx_parts.append(du * step_h + head_ref[h : h + 1, 2:3] * dy_h)
        dstep_cols.append(jnp.sum(x_h * du, axis=1, keepdims=True))
        dcum_cols.append(jnp.sum(dy_h * ssm_ref[:, cols] - u_h * du, axis=1, keepdims=True))
        dskips.append(jnp.sum(jnp.sum(dy_h * x_h, axis=1, keepdims=True), axis=0, keepdims=True))
    dx_act = jnp.concatenate(dx_parts, axis=1)
    blank = jnp.zeros((length, 1), F32)
    flat = jnp.concatenate(
        dcum_cols + [blank] * (8 - heads) + dstep_cols + [blank] * (8 - heads), axis=1
    ).T
    dcum, dstep = flat[:8], flat[8:]
    at_least = lax.broadcasted_iota(jnp.int32, (length, length), 0) >= lax.broadcasted_iota(
        jnp.int32, (length, length), 1
    )
    drate = dot_nn(dcum, at_least.astype(F32), highest)
    pre, step, rate, _ = steps_and_sums(step_ref[...], head_ref, heads, False)
    dpre = (dstep - drate * jnp.exp(head_ref[:, 1:2])) * jax.nn.sigmoid(pre)
    dstep_low = dpre.astype(LOW)
    small[...] = jnp.zeros_like(small)
    small[0:1, :] = grad_gain_two
    small[1 : 1 + heads, :] = dot_nn(dstep_low, mixer_in)[:heads]
    head_row = 1 + heads + KCONV
    small[head_row : head_row + heads, 0:128] = jnp.broadcast_to(
        jnp.sum(drate * rate, axis=1, keepdims=True)[:heads], (heads, 128)
    )
    small[head_row : head_row + heads, 128:256] = jnp.broadcast_to(
        jnp.sum(dpre, axis=1, keepdims=True)[:heads], (heads, 128)
    )
    small[head_row : head_row + heads, 256:384] = jnp.broadcast_to(jnp.concatenate(dskips, axis=0), (heads, 128))

    dconv = dx_act * silu_slope(x_conv)
    dx, dtaps = convolve_back(dconv, x_ref[...].astype(F32), taps_ref.at[:, 2 * NS :], col_ref)
    back_ref[:, HD + width :] = dx.astype(LOW)
    small[1 + heads : head_row, 2 * NS : 2 * NS + width] = dtaps
    for index, grad, conv in (
        (0, dot_tn(dmeet, cstate, highest), bconv),
        (1, dot_nn(dmeet, bstate, highest), cconv),
    ):
        lanes = slice(index * NS, (index + 1) * NS)
        grad_in, dtaps = convolve_back(
            grad * silu_slope(conv), kv_ref[2 + index].astype(F32), taps_ref.at[:, lanes], col_ref
        )
        aux_send[2 + index] = grad_in.astype(LOW)
        small[1 + heads : head_row, lanes] = dtaps

    to = plane_order()
    aux_copies = [
        send(aux_send.at[to[k]], aux_recv.at[k], aux_sem.at[0, k], aux_sem.at[1, k], seq_peers[k - 1])
        for k in (1, 2, 3)
    ]
    small_dp = dp_sends(dp_count, lambda j: small, lambda k: small_came.at[k], dp_sem, 16)
    gs_entry[...] = dot_tn(mixer_in, back_ref[...]).astype(LOW)
    entry_red = reduce_begin(gs_entry, gr_entry, 12)
    aux_sum = aux_send[s].astype(F32)
    for k in (1, 2, 3):
        aux_copies[k - 1].wait_recv()
        aux_sum = aux_sum + aux_recv[k].astype(F32)
    aux_near[0] = aux_sum.astype(LOW)
    pair = send(aux_near.at[0], aux_near.at[1], aux_sem.at[0, 0], aux_sem.at[1, 0], other)
    input_part = (
        dot_nt(back_ref[:, :HD], entry_w[:, :HD])
        + dot_nt(back_ref[:, HD:], entry_w[:, 2 * HD :])
        + dot_tn(dstep_low, step_w)
    )
    both = jnp.where(s >= 2, 1.0, 0.0)
    once = jnp.where(t == 0, 1.0, 1.0 - both)
    pair.wait_recv()
    daux = (aux_sum + both * aux_near[1].astype(F32)).astype(LOW)
    daux_once = (daux.astype(F32) * once).astype(LOW)
    rounded_part(part.at[3], input_part + dot_nt(daux_once, entry_w[:, HD : 2 * HD]))
    in_near = begin(3)
    gs_aux[...] = dot_tn(mixer_in, daux).astype(LOW)
    aux_red = reduce_begin(gs_aux, gr_aux, 14)
    in_far = middle_of(3, in_near)

    out_ref[t] = middle_ref[...] + end(2, out_near, out_far)
    out_pair = send(out_ref.at[t], out_ref.at[t], kv_sem.at[0, 3], kv_sem.at[1, 3], other)
    small_total = small[...]
    for k in range(1, dp_count):
        small_dp[k - 1].wait_recv()
        small_total = small_total + small_came[k]
    index = 2 * s + t
    small_all[index] = small_total
    small_plane = [
        send(small_all.at[index], small_all.at[index], small_sem.at[0, i], small_sem.at[1, i], peer)
        for i, peer in enumerate(peers)
    ]
    grad_hidden, grad_gain_one = norm_backward(end(3, in_near, in_far), hid_ref[...], gain_one, grad_ref[...])
    hid_grad_ref[t] = grad_hidden
    hid_pair = send(hid_grad_ref.at[t], hid_grad_ref.at[t], aux_sem.at[0, 4], aux_sem.at[1, 4], other)
    gain[...] = jnp.broadcast_to(grad_gain_one, gain.shape)
    gain_dp = dp_sends(dp_count, lambda j: gain, lambda k: gain_came.at[k], dp_sem, 18)
    finals = reduce_end(gs_feed, gr_feed, fin_feed, feed_red, 0)
    finals += reduce_end(gs_outs, gr_outs, fin_outs, outs_red, 1)
    gain_total = gain[...]
    for k in range(1, dp_count):
        gain_dp[k - 1].wait_recv()
        gain_total = gain_total + gain_came[k]
    gain_all[index] = gain_total
    gain_plane = [
        send(gain_all.at[index], gain_all.at[index], gain_sem.at[0, i], gain_sem.at[1, i], peer)
        for i, peer in enumerate(peers)
    ]
    finals += reduce_end(gs_entry, gr_entry, fin_entry, entry_red, 2)
    finals += reduce_end(gs_aux, gr_aux, fin_aux, aux_red, 3)
    for copy in (out_pair, hid_pair, *small_plane, *gain_plane, *finals):
        copy.wait_recv()
        copy.wait_send()
    for copy in (
        *spares, *entries, *outers, *feeds, *shared, *feed_red, *outs_red, *entry_red, *aux_red, *aux_copies, pair,
        *small_dp, *gain_dp,
    ):
        copy.wait_send()


def call(kernel, collective_id, outs, scratch, *operands, far=()):
    vmem = pl.BlockSpec(memory_space=pltpu.VMEM)
    in_specs = [pl.BlockSpec(memory_space=pl.ANY) if i in far else vmem for i in range(len(operands))]
    return pl.pallas_call(
        kernel,
        out_shape=[jax.ShapeDtypeStruct(shape, kind) for shape, kind in outs],
        in_specs=in_specs,
        out_specs=[vmem] * len(outs),
        scratch_shapes=scratch,
        compiler_params=pltpu.CompilerParams(
            collective_id=collective_id, has_side_effects=True, vmem_limit_bytes=56 * 2**20
        ),
    )(*operands)


def dma_sems(*counts):
    return [pltpu.SemaphoreType.DMA((count,)) for count in counts]


def rope_angles(token_pos, head_width):
    half_width = head_width // 2
    freq_index = jnp.arange(half_width, dtype=F32)
    inverse_freq = jnp.exp(freq_index * (-2.0 * math.log(rope_base) / head_width))
    angles = token_pos.astype(F32)[:, None] * inverse_freq[None, :]
    return (jnp.cos(angles), jnp.sin(angles))


def body(
    hidden_in,
    cotangent,
    segment_ids,
    positions,
    w_query,
    w_key,
    w_value,
    w_mamba_gate,
    w_mamba_in,
    w_mamba_bcdt,
    w_attention_out,
    w_mamba_out,
    w_feed_gate,
    w_feed_up,
    w_feed_down,
    gain_mixer,
    gain_feed,
    conv_weight,
    log_decay,
    step_bias,
    skip_scale,
):
    s, t, d = lax.axis_index("seq"), lax.axis_index("tensor"), lax.axis_index("dp")
    seq_count, tensor_count, dp_count = (
        lax.axis_size("seq"),
        lax.axis_size("tensor"),
        lax.axis_size("dp"),
    )
    length = segment_ids.shape[0]
    rows = hidden_in.shape[0] // tensor_count
    owner = w_query.shape[0]
    heads_dev = MH // (seq_count * tensor_count)
    width = heads_dev * MP
    group = t * seq_count + s
    score_scale = HD ** (-0.5)
    feed_width = w_feed_gate.shape[1] // seq_count

    def own(weight, size, dim):
        return lax.dynamic_slice_in_dim(weight, s * size, size, dim)

    aux = lax.select_n(
        s, w_key, w_value, w_mamba_bcdt[:, :NS], w_mamba_bcdt[:, NS : 2 * NS]
    )
    entry_own = jnp.concatenate(
        [own(w_query, HD, 1), aux, own(w_mamba_gate, width, 1), own(w_mamba_in, width, 1)], axis=1
    )
    outs_own = jnp.concatenate(
        [own(w_attention_out, HD, 0), own(w_feed_down, feed_width, 0), own(w_mamba_out, width, 0)],
        axis=0,
    ).T
    feed_own = jnp.concatenate([own(w_feed_gate, feed_width, 1), own(w_feed_up, feed_width, 1)], axis=1)
    step_cols = lax.dynamic_slice_in_dim(w_mamba_bcdt, 2 * NS + group * heads_dev, heads_dev, 1)
    spare = jnp.concatenate(
        [step_cols.T.astype(F32), gain_mixer[None].astype(F32), gain_feed[None].astype(F32)], axis=0
    )
    spare = lax.dynamic_update_slice(jnp.zeros((8, D), F32), spare, (0, d * owner))
    my_rows = lambda array: lax.dynamic_slice_in_dim(array, t * rows, rows, 0)
    hid_own, cot_own = my_rows(hidden_in), my_rows(cotangent)
    cosine, sine_vals = rope_angles(positions, HD)
    cos_table = jnp.concatenate([cosine, cosine], axis=1)
    sin_table = jnp.concatenate([-sine_vals, sine_vals], axis=1)
    row_meta = jnp.zeros((8, length), F32).at[:2].set(
        jnp.stack([segment_ids, positions]).astype(F32)
    )
    col_meta = row_meta.T
    conv_taps = jnp.concatenate(
        [conv_weight[:, MD:], lax.dynamic_slice_in_dim(conv_weight, group * width, width, 1)], axis=1
    )
    per_head = lambda vector: lax.dynamic_slice_in_dim(vector, group * heads_dev, heads_dev, 0)
    head_meta = jnp.zeros((8, 128), F32).at[:heads_dev, :3].set(
        jnp.stack([per_head(step_bias), per_head(log_decay), per_head(skip_scale)], axis=1)
    )
    n = dp_count
    vmem, total_rows = pltpu.VMEM, seq_count * tensor_count * rows
    sizes = (3 * feed_width, HD + width, HD + 2 * width, HD)
    out_two, hid_two, fin_feed, fin_outs, fin_entry, fin_aux, small_all, gain_all = call(
        functools.partial(layer_kernel, dp_count, heads_dev),
        1,
        [
            ((2, rows, D), F32),
            ((2, rows, D), F32),
            *[((seq_count, owner, size), LOW) for size in sizes],
            ((8, 16, D), F32),
            ((8, 8, D), F32),
        ],
        [
            vmem((n, 8, D), F32),
            vmem((length, 2 * D), LOW),
            vmem((length, D), LOW),
            vmem((length, D), LOW),
            vmem((D, entry_own.shape[1]), LOW),
            vmem((D, feed_own.shape[1]), LOW),
            vmem((D, outs_own.shape[1]), LOW),
            vmem((seq_count, length, HD), LOW),
            vmem((length, HD), LOW),
            vmem((length, width), F32),
            vmem((length, width), LOW),
            vmem((8, length), F32),
            vmem((length, HD + width), LOW),
            vmem((length, width), F32),
            vmem((length, length), F32),
            vmem((heads_dev, length, length), F32),
            vmem((length, length), F32),
            vmem((rows, D), F32),
            vmem((rows, D), F32),
            vmem((length, 2 * feed_width), LOW),
            vmem((length, feed_width), LOW),
            vmem((length, HD + 2 * width), LOW),
            vmem((4, seq_count, tensor_count, rows, D), LOW),
            *[vmem((4, 4, rows, D), LOW) for _ in range(3)],
            *[vmem((D, size), LOW) for size in sizes],
            *[vmem((n, owner, size), LOW) for size in sizes],
            vmem((seq_count, length, HD), LOW),
            vmem((4, length, HD), LOW),
            vmem((2, length, HD), LOW),
            vmem((16, D), F32),
            vmem((n, 16, D), F32),
            vmem((8, D), F32),
            vmem((n, 8, D), F32),
            pltpu.SemaphoreType.DMA((20, n)),
            pltpu.SemaphoreType.DMA((3,)),
            pltpu.SemaphoreType.DMA((7, 2, 8)),
            pltpu.SemaphoreType.DMA((4, 2, 3)),
            pltpu.SemaphoreType.DMA((2, 4)),
            pltpu.SemaphoreType.DMA((2, 5)),
            pltpu.SemaphoreType.DMA((2, 7)),
            pltpu.SemaphoreType.DMA((2, 7)),
        ],
        spare, hid_own, cot_own, entry_own, feed_own, outs_own, cos_table, sin_table, col_meta, row_meta, conv_taps, head_meta,
        far=(3, 4, 5),
    )
    output, grad_hidden = out_two.reshape(2 * rows, D), hid_two.reshape(2 * rows, D)

    small_all = small_all.reshape(seq_count, tensor_count, 16, D)
    cols_own = lambda array: lax.dynamic_slice_in_dim(array, d * owner, owner, array.ndim - 1)
    grad_gain_mixer = cols_own(jnp.sum(gain_all[:, 0], axis=0))
    grad_gain_feed = cols_own(jnp.sum(small_all[:, :, 0], axis=(0, 1)))
    by_group = small_all.transpose(1, 0, 2, 3).reshape(seq_count * tensor_count, 16, D)
    grad_step_w = cols_own(by_group[:, 1 : 1 + heads_dev]).reshape(MH, owner).T
    head_row = 1 + heads_dev + KCONV
    taps = by_group[:, 1 + heads_dev : head_row, : 2 * NS + width]
    grad_conv_weight = jnp.concatenate(
        [taps[:, :, 2 * NS :].transpose(1, 0, 2).reshape(KCONV, MD), jnp.sum(taps[:, :, : 2 * NS], axis=0)], axis=1
    )
    heads = by_group[:, head_row : head_row + heads_dev].reshape(MH, D)

    side = lambda blocks, low, high: jnp.concatenate(
        [blocks[i, :, low:high].astype(F32) for i in range(seq_count)], axis=1
    )
    below = lambda blocks, low, high: jnp.concatenate(
        [blocks[i, :, low:high].astype(F32).T for i in range(seq_count)], axis=0
    )
    return (
        output,
        grad_hidden,
        side(fin_entry, 0, HD),
        fin_aux[0].astype(F32),
        fin_aux[1].astype(F32),
        side(fin_entry, HD, HD + width),
        side(fin_entry, HD + width, HD + 2 * width),
        jnp.concatenate([fin_aux[2].astype(F32), fin_aux[3].astype(F32), grad_step_w], axis=1),
        below(fin_outs, 0, HD),
        below(fin_outs, HD, HD + width),
        side(fin_feed, 0, feed_width),
        side(fin_feed, feed_width, 2 * feed_width),
        below(fin_feed, 2 * feed_width, 3 * feed_width),
        grad_gain_mixer,
        grad_gain_feed,
        grad_conv_weight,
        heads[:, 0],
        heads[:, 128],
        heads[:, 256],
    )


def solution(mesh):
    return jax.shard_map(
        body,
        mesh=mesh,
        in_specs=(
            P(("dp", "seq"), None),
            P(("dp", "seq"), None),
            P("dp"),
            P("dp"),
            P("dp", "tensor"),
            P("dp", "tensor"),
            P("dp", "tensor"),
            P("dp", "tensor"),
            P("dp", "tensor"),
            P("dp", None),
            P("tensor", "dp"),
            P("tensor", "dp"),
            P("dp", "tensor"),
            P("dp", "tensor"),
            P("tensor", "dp"),
            P("dp"),
            P("dp"),
            P(),
            P(),
            P(),
            P(),
        ),
        out_specs=(
            P(("dp", "seq"), None),
            P(("dp", "seq"), None),
            P("dp", "tensor"),
            P("dp", "tensor"),
            P("dp", "tensor"),
            P("dp", "tensor"),
            P("dp", "tensor"),
            P("dp", None),
            P("tensor", "dp"),
            P("tensor", "dp"),
            P("dp", "tensor"),
            P("dp", "tensor"),
            P("tensor", "dp"),
            P("dp"),
            P("dp"),
            P(),
            P(),
            P(),
            P(),
        ),
        check_vma=False,
    )
```

```python
import functools
import math

import jax
import jax.numpy as jnp
from jax import lax
from jax.experimental import pallas as pl
from jax.experimental.pallas import tpu as pltpu
from jax.sharding import PartitionSpec as P

D = 1024
HD = 128
MH = 24
MP = 64
NS = 128
KCONV = 4
MD = 1536

MESH = pl.DeviceIdType.MESH
LOW = jnp.bfloat16
F32 = jnp.float32

epsilon = 1e-05
rope_base = 100000000000.0
masked_score = -1e30
highest = lax.Precision.HIGHEST


def seq_partner(seq_index, k):
    if k == 1:
        return seq_index + 1 - 2 * (seq_index % 2)
    if k == 2:
        return seq_index + 2 - 4 * (seq_index // 2)
    return 3 - seq_index


def greet(devices):
    barrier = pltpu.get_barrier_semaphore()
    for device in devices:
        pl.semaphore_signal(barrier, inc=1, device_id=device, device_id_type=MESH)
    pl.semaphore_wait(barrier, len(devices))


def plane_peers():
    s, t = lax.axis_index("seq"), lax.axis_index("tensor")
    return [{"seq": seq_partner(s, k), "tensor": t} for k in (1, 2, 3)] + [
        {"seq": s, "tensor": 1 - t}
    ]


def send(src, dst, send_sem, recv_sem, device):
    copy = pltpu.make_async_remote_copy(
        src_ref=src,
        dst_ref=dst,
        send_sem=send_sem,
        recv_sem=recv_sem,
        device_id=device,
        device_id_type=MESH,
    )
    copy.start()
    return copy


def spread_begin(out_ref, rows, sems):
    s, t = lax.axis_index("seq"), lax.axis_index("tensor")
    mine = out_ref.at[pl.ds(pl.multiple_of((2 * s + t) * rows, rows), rows)]
    devices = [{"seq": s, "tensor": 1 - t}] + [{"seq": seq_partner(s, k), "tensor": t} for k in (1, 2, 3)]
    return [send(mine, mine, sems.at[0, k], sems.at[1, k], devices[k]) for k in (1, 2, 3, 0)]


def spread_end(out_ref, rows, sems, copies):
    s, t = lax.axis_index("seq"), lax.axis_index("tensor")
    for k in (1, 2, 3):
        copies[k - 1].wait_recv()
        came = out_ref.at[pl.ds(pl.multiple_of((2 * seq_partner(s, k) + t) * rows, rows), rows)]
        copies.append(send(came, came, sems.at[0, 3 + k], sems.at[1, 3 + k], {"seq": s, "tensor": 1 - t}))
    for copy in copies[3:]:
        copy.wait_recv()
    for copy in copies:
        copy.wait_send()


def plane_order():
    s = lax.axis_index("seq")
    return [s, seq_partner(s, 1), seq_partner(s, 2), seq_partner(s, 3)]


def sum_begin(part_ref, near_ref, sems):
    s, t = lax.axis_index("seq"), lax.axis_index("tensor")
    to = plane_order()
    return {
        k: send(part_ref.at[to[k], 1 - t], near_ref.at[k], sems.at[0, k], sems.at[1, k], {"seq": s, "tensor": 1 - t})
        for k in (3, 1, 2, 0)
    }


def sum_middle(part_ref, near_ref, low_ref, far_ref, sems, near):
    t = lax.axis_index("tensor")
    to, far = plane_order(), {}
    for k in (3, 1, 2):
        near[k].wait_recv()
        low_ref[k] = (part_ref[to[k], t].astype(F32) + near_ref[k].astype(F32)).astype(LOW)
        far[k] = send(
            low_ref.at[k], far_ref.at[k], sems.at[0, 4 + k], sems.at[1, 4 + k], {"seq": to[k], "tensor": t}
        )
    return far


def sum_end(part_ref, near_ref, far_ref, near, far):
    s, t = lax.axis_index("seq"), lax.axis_index("tensor")
    near[0].wait_recv()
    total = part_ref[s, t].astype(F32) + near_ref[0].astype(F32)
    for k in (1, 2, 3):
        far[k].wait_recv()
        total = total + far_ref[k].astype(F32)
    for copy in (*near.values(), *far.values()):
        copy.wait_send()
    return total


def dot_nt(left, right, precision=None):
    return lax.dot_general(left, right, (((1,), (1,)), ((), ())), precision=precision, preferred_element_type=F32)


def dot_tn(left, right, precision=None):
    return lax.dot_general(left, right, (((0,), (0,)), ((), ())), precision=precision, preferred_element_type=F32)


def dot_nn(left, right, precision=None):
    return lax.dot_general(left, right, (((1,), (0,)), ((), ())), precision=precision, preferred_element_type=F32)


def turn(values, cos_ref, sin_ref):
    return values * cos_ref[...] + pltpu.roll(values, HD // 2, 1) * sin_ref[...]


def turn_back(values, cos_ref, sin_ref):
    return values * cos_ref[...] - pltpu.roll(values, HD // 2, 1) * sin_ref[...]


def visible(col_ref, row_ref):
    return (col_ref[:, 0:1] == row_ref[0:1, :]) & (row_ref[1:2, :] <= col_ref[:, 1:2])


def convolve(mixed, taps_ref, col_ref):
    total = taps_ref[0:1] * mixed
    for lag in range(1, KCONV):
        kept = jnp.where(col_ref[:, 1:2] >= lag, pltpu.roll(mixed, lag, 0), 0.0)
        total = total + taps_ref[lag : lag + 1] * kept
    return total


def steps_and_sums(raw, head_ref, heads, summed=True):
    raw = jnp.where(lax.broadcasted_iota(jnp.int32, raw.shape, 0) < heads, raw, 0.0)
    pre = raw + head_ref[:, 0:1]
    step = jnp.maximum(pre, 0.0) + jnp.log1p(jnp.exp(-jnp.abs(pre)))
    rate = -step * jnp.exp(head_ref[:, 1:2])
    if not summed:
        return pre, step, rate, None
    length = raw.shape[1]
    upto = lax.broadcasted_iota(jnp.int32, (length, length), 0) <= lax.broadcasted_iota(
        jnp.int32, (length, length), 1
    )
    return pre, step, rate, dot_nn(rate, upto.astype(F32), highest)


def when(condition, act):
    if condition is None:
        act()
    else:
        pl.when(condition)(act)


class Moves:
    def __init__(self, dp_count, sems, row, src_of, dst_of, relayed=False):
        d = lax.axis_index("dp")
        self.count, self.sems, self.row, self.d = dp_count, sems, row, d
        self.relayed = relayed and dp_count == 4
        self.copies = {
            k: self.make(src_of(lax.rem(d + k, dp_count)), dst_of(k), k, k, lax.rem(d + k, dp_count))
            for k in range(1, dp_count)
        }

    def make(self, src, dst, at, there, to):
        return pltpu.make_async_remote_copy(
            src_ref=src, dst_ref=dst, send_sem=self.sems.at[self.row, at], recv_sem=self.sems.at[self.row + 1, there],
            device_id={"dp": to}, device_id_type=MESH,
        )

    def direct(self, k):
        if not self.relayed or k == 2:
            return None
        return self.d != (3 if k == 1 else 0)

    def inner(self):
        return (self.d == 1) | (self.d == 2)

    def start(self):
        for k, copy in self.copies.items():
            when(self.direct(k), copy.start)
        return self


class Gather(Moves):
    def __init__(self, dp_count, sems, row, own, full, owner, relayed=True):
        d = lax.axis_index("dp")
        rows = lambda j: full.at[pl.ds(pl.multiple_of(j * owner, owner), owner)]
        super().__init__(dp_count, sems, row, lambda j: own, lambda k: rows(d), relayed)
        if self.relayed:
            far = rows(lax.rem(d + 2, 4))
            self.passed = self.make(far, far, 0, 2 * d - 1, 3 * (d - 1))

    def relay(self):
        if self.relayed:
            def act():
                self.copies[2].wait_recv()
                self.passed.start()

            when(self.inner(), act)

    def finish(self):
        for k, copy in self.copies.items():
            when(jnp.logical_not(self.inner()) if self.relayed and k == 2 else None, copy.wait_recv)

    def wait_send(self):
        for k, copy in self.copies.items():
            when(self.direct(k), copy.wait_send)
        if self.relayed:
            when(self.inner(), self.passed.wait_send)


class Reduce(Moves):
    def __init__(self, dp_count, sems, row, parts, came, owner, relayed=False):
        rows = lambda j: parts.at[pl.ds(pl.multiple_of(j * owner, owner), owner)]
        super().__init__(dp_count, sems, row, rows, lambda k: came.at[k], relayed)
        self.parts, self.came, self.owner = parts, came, owner
        passed = came.at[0]
        if self.relayed:
            self.turns = {1: self.make(rows(0), passed, 1, 0, 2), 3: self.make(rows(3), passed, 3, 0, 1)}

    def start(self):
        if not self.relayed:
            return super().start()
        for k in (1, 3):
            when(jnp.logical_not(self.direct(k)), self.turns[k].start)
        when(self.d == 0, lambda: self.blank(1))
        when(self.d == 3, lambda: self.blank(3))
        when(jnp.logical_not(self.inner()), self.copies[2].start)
        for k in (1, 3):
            when(self.direct(k), self.copies[k].start)
        return self

    def blank(self, k):
        self.came[k] = jnp.zeros(self.came.shape[1:], self.came.dtype)

    def relay(self):
        if self.relayed:
            def act():
                self.turns[1].wait_recv()
                at = pl.ds(pl.multiple_of(lax.rem(self.d + 2, 4) * self.owner, self.owner), self.owner)
                self.parts[at] = (self.parts[at].astype(F32) + self.came[0].astype(F32)).astype(LOW)
                self.copies[2].start()

            when(self.inner(), act)

    def total(self):
        at = pl.ds(pl.multiple_of(self.d * self.owner, self.owner), self.owner)
        value = self.parts[at].astype(F32)
        for k, copy in self.copies.items():
            absent = {1: 0, 3: 3}.get(k)
            when(self.d != absent if self.relayed and absent is not None else None, copy.wait_recv)
        for k in self.copies:
            value = value + self.came[k].astype(F32)
        return value

    def wait_send(self):
        for k, copy in self.copies.items():
            when(self.direct(k), copy.wait_send)
        if self.relayed:
            for k in (1, 3):
                when(jnp.logical_not(self.direct(k)), self.turns[k].wait_send)


class Share(Moves):
    def __init__(self, dp_count, sems, row, own, came):
        super().__init__(dp_count, sems, row, lambda j: own, lambda k: came.at[k])
        self.own, self.came = own, came

    def total(self):
        value = self.own[...]
        for k, copy in self.copies.items():
            copy.wait_recv()
            value = value + self.came[k]
        return value

    def wait_send(self):
        for copy in self.copies.values():
            copy.wait_send()


def convolve_back(grad, mixed, taps_ref, col_ref):
    length = grad.shape[0]
    total = taps_ref[0:1] * grad
    taps = [jnp.sum(grad * mixed, axis=0, keepdims=True)]
    for lag in range(1, KCONV):
        kept = jnp.where(col_ref[:, 1:2] >= lag, grad, 0.0)
        total = total + taps_ref[lag : lag + 1] * pltpu.roll(kept, length - lag, 0)
        taps.append(jnp.sum(kept * pltpu.roll(mixed, lag, 0), axis=0, keepdims=True))
    return total, jnp.concatenate(taps, axis=0)


def norm_backward(grad, values, gain, upstream):
    scale = lax.rsqrt(jnp.mean(values * values, axis=1, keepdims=True) + epsilon)
    normed = values * scale
    grad_gain = jnp.sum(grad * normed, axis=0, keepdims=True)
    inner = grad * gain
    result = upstream + scale * (inner - normed * jnp.mean(inner * normed, axis=1, keepdims=True))
    return result, grad_gain


def silu_slope(pre_act):
    sigmoid_gate = jax.nn.sigmoid(pre_act)
    return sigmoid_gate * (1.0 + pre_act * (1.0 - sigmoid_gate))


def rounded_part(part_ref, value):
    part_ref[...] = value.astype(LOW).reshape(part_ref.shape)


def layer_kernel(
    dp_count, heads,
    spare_ref, hid_ref, cot_ref, entry_own, feed_own, outs_own, cos_ref, sin_ref, col_ref, row_ref, taps_ref, head_ref,
    out_ref, hid_grad_ref, fin_feed, fin_outs, fin_entry, fin_x, fin_aux, small_all, gain_all,
    came, tok_ref, feed_ref, low_ref, entry_w, feed_w, outs_w, kv_ref, query_ref, gate_ref, x_ref, step_ref, mixed_ref,
    ssm_ref, prob_ref, decay_ref, meet_ref, middle_ref, grad_ref, dboth_ref, act_ref, back_ref,
    part, near, low, far, gs_feed, gs_outs, gs_entry, gs_x, gs_aux, gr_feed, gr_outs, gr_entry, gr_x, gr_aux,
    aux_send, aux_recv, aux_near, small, small_came, gain, gain_came,
    dp_sem, local, plane_sem, fin_sem, kv_sem, aux_sem, small_sem, gain_sem,
):
    d, s, t = lax.axis_index("dp"), lax.axis_index("seq"), lax.axis_index("tensor")
    rows, owner, width = hid_ref.shape[0], entry_own.shape[0], heads * MP
    length = tok_ref.shape[0]
    other = {"seq": s, "tensor": 1 - t}
    peers = []
    for k in range(4):
        for flip in range(2):
            if k or flip:
                peers.append({"seq": s if k == 0 else seq_partner(s, k), "tensor": 1 - t if flip else t})
    seq_peers = [{"seq": seq_partner(s, k), "tensor": t} for k in (1, 2, 3)]
    greet(peers + [{"dp": lax.rem(d + k, dp_count)} for k in range(1, dp_count)])
    place = pl.ds(pl.multiple_of(d * owner, owner), owner)
    spares = Share(dp_count, dp_sem, 0, spare_ref, came).start()
    entries = Gather(dp_count, dp_sem, 2, entry_own, entry_w, owner).start()
    locals_ = [
        pltpu.make_async_copy(own, full.at[place], local.at[i])
        for i, (own, full) in enumerate(((entry_own, entry_w), (feed_own, feed_w), (outs_own, outs_w)))
    ]
    for copy in locals_:
        copy.start()
    hid = hid_ref[...]
    normed = hid * lax.rsqrt(jnp.mean(hid * hid, axis=1, keepdims=True) + epsilon)
    total = spares.total()
    gain_one, gain_two, step_w = total[3:4], total[4:5], total.astype(LOW)
    mine = pl.ds(pl.multiple_of((2 * s + t) * rows, rows), rows)
    tok_ref[mine, :D] = (normed * gain_one).astype(LOW)
    tok_ref[mine, D:] = cot_ref[...].astype(LOW)
    spread_end(tok_ref, rows, plane_sem.at[0], spread_begin(tok_ref, rows, plane_sem.at[0]))
    entries.relay()
    outers = Gather(dp_count, dp_sem, 4, outs_own, outs_w, owner).start()
    entries.finish()
    feeds = Gather(dp_count, dp_sem, 6, feed_own, feed_w, owner).start()
    for copy in locals_:
        copy.wait()

    mixer_in = tok_ref[:, :D]
    aux = dot_nn(mixer_in, entry_w[:, HD : 2 * HD])
    is_key = jnp.where(s == 0, 1.0, 0.0)
    aux = turn(aux, cos_ref, sin_ref) * is_key + aux * (1.0 - is_key)
    kv_ref[s] = aux.astype(LOW)
    shared = [
        send(kv_ref.at[s], kv_ref.at[s], kv_sem.at[0, i], kv_sem.at[1, i], peer)
        for i, peer in enumerate(seq_peers)
    ]
    query_ref[...] = turn(dot_nn(mixer_in, entry_w[:, :HD]), cos_ref, sin_ref).astype(LOW)
    gate_x = dot_nn(mixer_in, entry_w[:, 2 * HD :])
    gate_ref[...] = gate_x[:, :width]
    x_ref[...] = gate_x[:, width:].astype(LOW)
    step_ref[...] = dot_nt(step_w, mixer_in).astype(LOW).astype(F32)
    _, step, _, cum = steps_and_sums(step_ref[...], head_ref, heads)
    columns = jnp.concatenate([cum, step], axis=0).T
    cum_col, step_col = columns[:, :8], columns[:, 8:]
    x_conv = convolve(x_ref[...].astype(F32), taps_ref.at[:, 2 * NS :], col_ref)
    x_act = x_conv * jax.nn.sigmoid(x_conv)
    allowed = visible(col_ref, row_ref)
    for copy in shared:
        copy.wait_recv()

    scores = jnp.where(allowed, dot_nt(query_ref[...], kv_ref[0]) * HD ** (-0.5), masked_score)
    peak = jnp.max(scores, axis=1, keepdims=True)
    logsum = peak + jnp.log(jnp.sum(jnp.exp(scores - peak), axis=1, keepdims=True))
    probs = jnp.exp(scores - logsum)
    prob_ref[...] = probs
    mixed_ref[:, :HD] = dot_nn(probs.astype(LOW), kv_ref[1]).astype(LOW)

    outers.relay()

    def state(index):
        conv = convolve(kv_ref[2 + index].astype(F32), taps_ref.at[:, index * NS : (index + 1) * NS], col_ref)
        return conv

    bconv, cconv = state(0), state(1)
    bstate, cstate = bconv * jax.nn.sigmoid(bconv), cconv * jax.nn.sigmoid(cconv)
    meet_ref[...] = dot_nt(cstate, bstate, highest)
    sums = []
    for h in range(heads):
        decay = jnp.exp(jnp.where(allowed, cum_col[:, h : h + 1] - cum[h : h + 1, :], masked_score))
        decay_ref[h] = decay
        x_head = x_act[:, h * MP : (h + 1) * MP]
        sums.append(dot_nn(meet_ref[...] * decay, x_head * step_col[:, h : h + 1], highest))
    core_out = jnp.concatenate(sums, axis=1)
    skips = jnp.concatenate(
        [jnp.broadcast_to(head_ref[h : h + 1, 2:3], (1, MP)) for h in range(heads)], axis=1
    )
    ssm_ref[...] = core_out
    ssm_low = (core_out + skips * x_act).astype(LOW).astype(F32)
    gate_pre = gate_ref[...]
    mixed_ref[:, HD:] = (ssm_low * (gate_pre * jax.nn.sigmoid(gate_pre))).astype(LOW)

    outers.finish()
    down_start = HD + act_ref.shape[1]
    rounded_part(
        part.at[0],
        dot_nt(mixed_ref[:, :HD], outs_w[:, :HD]) + dot_nt(mixed_ref[:, HD:], outs_w[:, down_start:]),
    )

    def begin(i):
        return sum_begin(part.at[i % 3], near.at[i % 3], plane_sem.at[1 + i])

    def middle_of(i, copies):
        return sum_middle(part.at[i % 3], near.at[i % 3], low.at[i % 3], far.at[i % 3], plane_sem.at[1 + i], copies)

    def end(i, copies, later):
        return sum_end(part.at[i % 3], near.at[i % 3], far.at[i % 3], copies, later)

    sum_near = begin(0)
    feeds.relay()
    middle = hid_ref[...] + end(0, sum_near, middle_of(0, sum_near))
    middle_ref[...] = middle
    scale = lax.rsqrt(jnp.mean(middle * middle, axis=1, keepdims=True) + epsilon)
    feed_ref[mine, :] = (middle * scale * gain_two).astype(LOW)
    spread_end(feed_ref, rows, plane_sem.at[5], spread_begin(feed_ref, rows, plane_sem.at[5]))
    feeds.finish()

    half = act_ref.shape[1]
    feed_gate = dot_nn(feed_ref[...], feed_w[:, :half])
    feed_up = dot_nn(feed_ref[...], feed_w[:, half:])
    feed_sig = jax.nn.sigmoid(feed_gate)
    feed_silu = feed_gate * feed_sig
    act_ref[...] = (feed_silu * feed_up).astype(LOW)
    grad_act = dot_nn(tok_ref[:, D:], outs_w[:, HD:down_start])
    dboth_ref[:, :half] = (grad_act * feed_up * (feed_sig * (1.0 + feed_gate * (1.0 - feed_sig)))).astype(LOW)
    dboth_ref[:, half:] = (grad_act * feed_silu).astype(LOW)
    rounded_part(part.at[1], dot_nt(dboth_ref[...], feed_w[...]))
    sum_near = begin(1)
    gs_feed[:, : 2 * half] = dot_tn(feed_ref[...], dboth_ref[...]).astype(LOW)
    sum_far = middle_of(1, sum_near)
    gs_feed[:, 2 * half :] = dot_tn(tok_ref[:, D:], act_ref[...]).astype(LOW)

    def publish(reduce, fin, row):
        fin[s] = reduce.total().astype(LOW)
        return [
            send(fin.at[s], fin.at[s], fin_sem.at[row, 0, i], fin_sem.at[row, 1, i], peer)
            for i, peer in enumerate(seq_peers)
        ]

    feed_red = Reduce(dp_count, dp_sem, 8, gs_feed, gr_feed, owner, True).start()
    grad_middle, grad_gain_two = norm_backward(end(1, sum_near, sum_far), middle_ref[...], gain_two, cot_ref[...])
    grad_ref[...] = grad_middle
    low_ref[mine, :] = grad_middle.astype(LOW)
    spread = spread_begin(low_ref, rows, plane_sem.at[6])
    rounded_part(part.at[2], dot_nt(act_ref[...], outs_w[:, HD:down_start]))
    spread_end(low_ref, rows, plane_sem.at[6], spread)
    out_near = begin(2)

    grad_gated = dot_nn(low_ref[...], outs_w[:, down_start:])
    grad_attended = dot_nn(low_ref[...], outs_w[:, :HD]).astype(LOW)
    gs_outs[...] = dot_tn(low_ref[...], mixed_ref[...]).astype(LOW)
    outs_red = Reduce(dp_count, dp_sem, 10, gs_outs, gr_outs, owner, True).start()
    gate_sig = jax.nn.sigmoid(gate_pre)
    back_ref[:, HD : HD + width] = (
        grad_gated * ssm_low * (gate_sig * (1.0 + gate_pre * (1.0 - gate_sig)))
    ).astype(LOW)
    dy = (grad_gated * (gate_pre * gate_sig)).astype(LOW).astype(F32)

    row_delta = jnp.sum(grad_attended.astype(F32) * mixed_ref[:, :HD].astype(F32), axis=1, keepdims=True)
    probs = prob_ref[...]
    aux_send[1] = dot_tn(probs.astype(LOW), grad_attended).astype(LOW)
    dscores = (probs * (dot_nt(grad_attended, kv_ref[1]) - row_delta)).astype(LOW)
    back_ref[:, :HD] = turn_back(dot_nn(dscores, kv_ref[0]) * HD ** (-0.5), cos_ref, sin_ref).astype(LOW)
    aux_send[0] = turn_back(dot_tn(dscores, query_ref[...]) * HD ** (-0.5), cos_ref, sin_ref).astype(LOW)
    out_far = middle_of(2, out_near)
    gs_entry[...] = dot_tn(mixer_in, back_ref[:, : HD + width]).astype(LOW)
    entry_red = Reduce(dp_count, dp_sem, 12, gs_entry, gr_entry, owner, True).start()
    feed_red.relay()

    dmeet = jnp.zeros((length, length), F32)
    dx_parts, dcum_cols, dstep_cols, dskips = [], [], [], []
    for h in range(heads):
        cols = slice(h * MP, (h + 1) * MP)
        step_h = step_col[:, h : h + 1]
        dy_h, x_h = dy[:, cols], x_act[:, cols]
        u_h = x_h * step_h
        du = dot_tn(meet_ref[...] * decay_ref[h], dy_h, highest)
        dmeet = dmeet + dot_nt(dy_h, u_h, highest) * decay_ref[h]
        dx_parts.append(du * step_h + head_ref[h : h + 1, 2:3] * dy_h)
        dstep_cols.append(jnp.sum(x_h * du, axis=1, keepdims=True))
        dcum_cols.append(jnp.sum(dy_h * ssm_ref[:, cols] - u_h * du, axis=1, keepdims=True))
        dskips.append(jnp.sum(jnp.sum(dy_h * x_h, axis=1, keepdims=True), axis=0, keepdims=True))
    dx_act = jnp.concatenate(dx_parts, axis=1)
    outs_red.relay()
    finals = publish(feed_red, fin_feed, 0)
    blank = jnp.zeros((length, 1), F32)
    flat = jnp.concatenate(
        dcum_cols + [blank] * (8 - heads) + dstep_cols + [blank] * (8 - heads), axis=1
    ).T
    dcum, dstep = flat[:8], flat[8:]
    at_least = lax.broadcasted_iota(jnp.int32, (length, length), 0) >= lax.broadcasted_iota(
        jnp.int32, (length, length), 1
    )
    drate = dot_nn(dcum, at_least.astype(F32), highest)
    pre, step, rate, _ = steps_and_sums(step_ref[...], head_ref, heads, False)
    dpre = (dstep - drate * jnp.exp(head_ref[:, 1:2])) * jax.nn.sigmoid(pre)
    dstep_low = dpre.astype(LOW)
    small[...] = jnp.zeros_like(small)
    small[0:1, :] = grad_gain_two
    small[1 : 1 + heads, :] = dot_nn(dstep_low, mixer_in)[:heads]
    head_row = 1 + heads + KCONV
    small[head_row : head_row + heads, 0:128] = jnp.broadcast_to(
        jnp.sum(drate * rate, axis=1, keepdims=True)[:heads], (heads, 128)
    )
    small[head_row : head_row + heads, 128:256] = jnp.broadcast_to(
        jnp.sum(dpre, axis=1, keepdims=True)[:heads], (heads, 128)
    )
    small[head_row : head_row + heads, 256:384] = jnp.broadcast_to(jnp.concatenate(dskips, axis=0), (heads, 128))

    dconv = dx_act * silu_slope(x_conv)
    dx, dtaps = convolve_back(dconv, x_ref[...].astype(F32), taps_ref.at[:, 2 * NS :], col_ref)
    back_ref[:, HD + width :] = dx.astype(LOW)
    small[1 + heads : head_row, 2 * NS : 2 * NS + width] = dtaps
    for index, grad, conv in (
        (0, dot_tn(dmeet, cstate, highest), bconv),
        (1, dot_nn(dmeet, bstate, highest), cconv),
    ):
        lanes = slice(index * NS, (index + 1) * NS)
        grad_in, dtaps = convolve_back(
            grad * silu_slope(conv), kv_ref[2 + index].astype(F32), taps_ref.at[:, lanes], col_ref
        )
        aux_send[2 + index] = grad_in.astype(LOW)
        small[1 + heads : head_row, lanes] = dtaps

    to = plane_order()
    aux_copies = [
        send(aux_send.at[to[k]], aux_recv.at[k], aux_sem.at[0, k], aux_sem.at[1, k], seq_peers[k - 1])
        for k in (1, 2, 3)
    ]
    small_dp = Share(dp_count, dp_sem, 16, small, small_came).start()
    gs_x[...] = dot_tn(mixer_in, back_ref[:, HD + width :]).astype(LOW)
    x_red = Reduce(dp_count, dp_sem, 20, gs_x, gr_x, owner).start()
    entry_red.relay()
    aux_sum = aux_send[s].astype(F32)
    for k in (1, 2, 3):
        aux_copies[k - 1].wait_recv()
        aux_sum = aux_sum + aux_recv[k].astype(F32)
    aux_near[0] = aux_sum.astype(LOW)
    pair = send(aux_near.at[0], aux_near.at[1], aux_sem.at[0, 0], aux_sem.at[1, 0], other)
    input_part = (
        dot_nt(back_ref[:, :HD], entry_w[:, :HD])
        + dot_nt(back_ref[:, HD:], entry_w[:, 2 * HD :])
        + dot_tn(dstep_low, step_w)
    )
    both = jnp.where(s >= 2, 1.0, 0.0)
    once = jnp.where(t == 0, 1.0, 1.0 - both)
    pair.wait_recv()
    daux = (aux_sum + both * aux_near[1].astype(F32)).astype(LOW)
    daux_once = (daux.astype(F32) * once).astype(LOW)
    rounded_part(part.at[0], input_part + dot_nt(daux_once, entry_w[:, HD : 2 * HD]))
    in_near = begin(3)
    gs_aux[...] = dot_tn(mixer_in, daux).astype(LOW)
    aux_red = Reduce(dp_count, dp_sem, 14, gs_aux, gr_aux, owner).start()
    in_far = middle_of(3, in_near)
    finals += publish(outs_red, fin_outs, 1)

    out_ref[t] = middle_ref[...] + end(2, out_near, out_far)
    out_pair = send(out_ref.at[t], out_ref.at[t], kv_sem.at[0, 3], kv_sem.at[1, 3], other)
    index = 2 * s + t
    small_all[index] = small_dp.total()
    small_plane = [
        send(small_all.at[index], small_all.at[index], small_sem.at[0, i], small_sem.at[1, i], peer)
        for i, peer in enumerate(peers)
    ]
    grad_hidden, grad_gain_one = norm_backward(end(3, in_near, in_far), hid_ref[...], gain_one, grad_ref[...])
    hid_grad_ref[t] = grad_hidden
    hid_pair = send(hid_grad_ref.at[t], hid_grad_ref.at[t], aux_sem.at[0, 4], aux_sem.at[1, 4], other)
    gain[...] = jnp.broadcast_to(grad_gain_one, gain.shape)
    gain_dp = Share(dp_count, dp_sem, 18, gain, gain_came).start()
    finals += publish(entry_red, fin_entry, 2)
    gain_all[index] = gain_dp.total()
    gain_plane = [
        send(gain_all.at[index], gain_all.at[index], gain_sem.at[0, i], gain_sem.at[1, i], peer)
        for i, peer in enumerate(peers)
    ]
    finals += publish(x_red, fin_x, 3)
    finals += publish(aux_red, fin_aux, 4)
    for copy in (out_pair, hid_pair, *small_plane, *gain_plane, *finals):
        copy.wait_recv()
        copy.wait_send()
    for copy in (
        spares, entries, outers, feeds, *shared, feed_red, outs_red, entry_red, x_red, aux_red, *aux_copies, pair,
        small_dp, gain_dp,
    ):
        copy.wait_send()


def call(kernel, collective_id, outs, scratch, *operands, far=()):
    vmem = pl.BlockSpec(memory_space=pltpu.VMEM)
    in_specs = [pl.BlockSpec(memory_space=pl.ANY) if i in far else vmem for i in range(len(operands))]
    return pl.pallas_call(
        kernel,
        out_shape=[jax.ShapeDtypeStruct(shape, kind) for shape, kind in outs],
        in_specs=in_specs,
        out_specs=[vmem] * len(outs),
        scratch_shapes=scratch,
        compiler_params=pltpu.CompilerParams(
            collective_id=collective_id, has_side_effects=True, vmem_limit_bytes=60 * 2**20
        ),
    )(*operands)


def dma_sems(*counts):
    return [pltpu.SemaphoreType.DMA((count,)) for count in counts]


def rope_angles(token_pos, head_width):
    half_width = head_width // 2
    freq_index = jnp.arange(half_width, dtype=F32)
    inverse_freq = jnp.exp(freq_index * (-2.0 * math.log(rope_base) / head_width))
    angles = token_pos.astype(F32)[:, None] * inverse_freq[None, :]
    return (jnp.cos(angles), jnp.sin(angles))


def body(
    hidden_in,
    cotangent,
    segment_ids,
    positions,
    w_query,
    w_key,
    w_value,
    w_mamba_gate,
    w_mamba_in,
    w_mamba_bcdt,
    w_attention_out,
    w_mamba_out,
    w_feed_gate,
    w_feed_up,
    w_feed_down,
    gain_mixer,
    gain_feed,
    conv_weight,
    log_decay,
    step_bias,
    skip_scale,
):
    s, t, d = lax.axis_index("seq"), lax.axis_index("tensor"), lax.axis_index("dp")
    seq_count, tensor_count, dp_count = (
        lax.axis_size("seq"),
        lax.axis_size("tensor"),
        lax.axis_size("dp"),
    )
    length = segment_ids.shape[0]
    rows = hidden_in.shape[0] // tensor_count
    owner = w_query.shape[0]
    heads_dev = MH // (seq_count * tensor_count)
    width = heads_dev * MP
    group = t * seq_count + s
    score_scale = HD ** (-0.5)
    feed_width = w_feed_gate.shape[1] // seq_count

    def own(weight, size, dim):
        return lax.dynamic_slice_in_dim(weight, s * size, size, dim)

    aux = lax.select_n(
        s, w_key, w_value, w_mamba_bcdt[:, :NS], w_mamba_bcdt[:, NS : 2 * NS]
    )
    entry_own = jnp.concatenate(
        [own(w_query, HD, 1), aux, own(w_mamba_gate, width, 1), own(w_mamba_in, width, 1)], axis=1
    )
    outs_own = jnp.concatenate(
        [own(w_attention_out, HD, 0), own(w_feed_down, feed_width, 0), own(w_mamba_out, width, 0)],
        axis=0,
    ).T
    feed_own = jnp.concatenate([own(w_feed_gate, feed_width, 1), own(w_feed_up, feed_width, 1)], axis=1)
    step_cols = lax.dynamic_slice_in_dim(w_mamba_bcdt, 2 * NS + group * heads_dev, heads_dev, 1)
    spare = jnp.concatenate(
        [step_cols.T.astype(F32), gain_mixer[None].astype(F32), gain_feed[None].astype(F32)], axis=0
    )
    spare = lax.dynamic_update_slice(jnp.zeros((8, D), F32), spare, (0, d * owner))
    my_rows = lambda array: lax.dynamic_slice_in_dim(array, t * rows, rows, 0)
    hid_own, cot_own = my_rows(hidden_in), my_rows(cotangent)
    cosine, sine_vals = rope_angles(positions, HD)
    cos_table = jnp.concatenate([cosine, cosine], axis=1)
    sin_table = jnp.concatenate([-sine_vals, sine_vals], axis=1)
    row_meta = jnp.zeros((8, length), F32).at[:2].set(
        jnp.stack([segment_ids, positions]).astype(F32)
    )
    col_meta = row_meta.T
    conv_taps = jnp.concatenate(
        [conv_weight[:, MD:], lax.dynamic_slice_in_dim(conv_weight, group * width, width, 1)], axis=1
    )
    per_head = lambda vector: lax.dynamic_slice_in_dim(vector, group * heads_dev, heads_dev, 0)
    head_meta = jnp.zeros((8, 128), F32).at[:heads_dev, :3].set(
        jnp.stack([per_head(step_bias), per_head(log_decay), per_head(skip_scale)], axis=1)
    )
    n = dp_count
    vmem, total_rows = pltpu.VMEM, seq_count * tensor_count * rows
    sizes = (3 * feed_width, HD + width, HD + width, width, HD)
    out_two, hid_two, fin_feed, fin_outs, fin_entry, fin_x, fin_aux, small_all, gain_all = call(
        functools.partial(layer_kernel, dp_count, heads_dev),
        1,
        [
            ((2, rows, D), F32),
            ((2, rows, D), F32),
            *[((seq_count, owner, size), LOW) for size in sizes],
            ((8, 16, D), F32),
            ((8, 8, D), F32),
        ],
        [
            vmem((n, 8, D), F32),
            vmem((length, 2 * D), LOW),
            vmem((length, D), LOW),
            vmem((length, D), LOW),
            vmem((D, entry_own.shape[1]), LOW),
            vmem((D, feed_own.shape[1]), LOW),
            vmem((D, outs_own.shape[1]), LOW),
            vmem((seq_count, length, HD), LOW),
            vmem((length, HD), LOW),
            vmem((length, width), F32),
            vmem((length, width), LOW),
            vmem((8, length), F32),
            vmem((length, HD + width), LOW),
            vmem((length, width), F32),
            vmem((length, length), F32),
            vmem((heads_dev, length, length), F32),
            vmem((length, length), F32),
            vmem((rows, D), F32),
            vmem((rows, D), F32),
            vmem((length, 2 * feed_width), LOW),
            vmem((length, feed_width), LOW),
            vmem((length, HD + 2 * width), LOW),
            vmem((3, seq_count, tensor_count, rows, D), LOW),
            *[vmem((3, 4, rows, D), LOW) for _ in range(3)],
            *[vmem((D, size), LOW) for size in sizes],
            *[vmem((n, owner, size), LOW) for size in sizes],
            vmem((seq_count, length, HD), LOW),
            vmem((4, length, HD), LOW),
            vmem((2, length, HD), LOW),
            vmem((16, D), F32),
            vmem((n, 16, D), F32),
            vmem((8, D), F32),
            vmem((n, 8, D), F32),
            pltpu.SemaphoreType.DMA((22, n)),
            pltpu.SemaphoreType.DMA((3,)),
            pltpu.SemaphoreType.DMA((7, 2, 8)),
            pltpu.SemaphoreType.DMA((5, 2, 3)),
            pltpu.SemaphoreType.DMA((2, 4)),
            pltpu.SemaphoreType.DMA((2, 5)),
            pltpu.SemaphoreType.DMA((2, 7)),
            pltpu.SemaphoreType.DMA((2, 7)),
        ],
        spare, hid_own, cot_own, entry_own, feed_own, outs_own, cos_table, sin_table, col_meta, row_meta, conv_taps, head_meta,
        far=(3, 4, 5),
    )
    output, grad_hidden = out_two.reshape(2 * rows, D), hid_two.reshape(2 * rows, D)

    small_all = small_all.reshape(seq_count, tensor_count, 16, D)
    cols_own = lambda array: lax.dynamic_slice_in_dim(array, d * owner, owner, array.ndim - 1)
    grad_gain_mixer = cols_own(jnp.sum(gain_all[:, 0], axis=0))
    grad_gain_feed = cols_own(jnp.sum(small_all[:, :, 0], axis=(0, 1)))
    by_group = small_all.transpose(1, 0, 2, 3).reshape(seq_count * tensor_count, 16, D)
    grad_step_w = cols_own(by_group[:, 1 : 1 + heads_dev]).reshape(MH, owner).T
    head_row = 1 + heads_dev + KCONV
    taps = by_group[:, 1 + heads_dev : head_row, : 2 * NS + width]
    grad_conv_weight = jnp.concatenate(
        [taps[:, :, 2 * NS :].transpose(1, 0, 2).reshape(KCONV, MD), jnp.sum(taps[:, :, : 2 * NS], axis=0)], axis=1
    )
    heads = by_group[:, head_row : head_row + heads_dev].reshape(MH, D)

    side = lambda blocks, low, high: jnp.concatenate(
        [blocks[i, :, low:high].astype(F32) for i in range(seq_count)], axis=1
    )
    below = lambda blocks, low, high: jnp.concatenate(
        [blocks[i, :, low:high].astype(F32).T for i in range(seq_count)], axis=0
    )
    return (
        output,
        grad_hidden,
        side(fin_entry, 0, HD),
        fin_aux[0].astype(F32),
        fin_aux[1].astype(F32),
        side(fin_entry, HD, HD + width),
        side(fin_x, 0, width),
        jnp.concatenate([fin_aux[2].astype(F32), fin_aux[3].astype(F32), grad_step_w], axis=1),
        below(fin_outs, 0, HD),
        below(fin_outs, HD, HD + width),
        side(fin_feed, 0, feed_width),
        side(fin_feed, feed_width, 2 * feed_width),
        below(fin_feed, 2 * feed_width, 3 * feed_width),
        grad_gain_mixer,
        grad_gain_feed,
        grad_conv_weight,
        heads[:, 0],
        heads[:, 128],
        heads[:, 256],
    )


def solution(mesh):
    return jax.shard_map(
        body,
        mesh=mesh,
        in_specs=(
            P(("dp", "seq"), None),
            P(("dp", "seq"), None),
            P("dp"),
            P("dp"),
            P("dp", "tensor"),
            P("dp", "tensor"),
            P("dp", "tensor"),
            P("dp", "tensor"),
            P("dp", "tensor"),
            P("dp", None),
            P("tensor", "dp"),
            P("tensor", "dp"),
            P("dp", "tensor"),
            P("dp", "tensor"),
            P("tensor", "dp"),
            P("dp"),
            P("dp"),
            P(),
            P(),
            P(),
            P(),
        ),
        out_specs=(
            P(("dp", "seq"), None),
            P(("dp", "seq"), None),
            P("dp", "tensor"),
            P("dp", "tensor"),
            P("dp", "tensor"),
            P("dp", "tensor"),
            P("dp", "tensor"),
            P("dp", None),
            P("tensor", "dp"),
            P("tensor", "dp"),
            P("dp", "tensor"),
            P("dp", "tensor"),
            P("tensor", "dp"),
            P("dp"),
            P("dp"),
            P(),
            P(),
            P(),
            P(),
        ),
        check_vma=False,
    )
```

```python
import functools
import math

import jax
import jax.numpy as jnp
from jax import lax
from jax.experimental import pallas as pl
from jax.experimental.pallas import tpu as pltpu
from jax.sharding import PartitionSpec as P

D = 1024
HD = 128
MH = 24
MP = 64
NS = 128
KCONV = 4
MD = 1536

MESH = pl.DeviceIdType.MESH
LOW = jnp.bfloat16
F32 = jnp.float32

epsilon = 1e-05
rope_base = 100000000000.0
masked_score = -1e30
highest = lax.Precision.HIGHEST


def seq_partner(seq_index, k):
    if k == 1:
        return seq_index + 1 - 2 * (seq_index % 2)
    if k == 2:
        return seq_index + 2 - 4 * (seq_index // 2)
    return 3 - seq_index


def greet(devices):
    barrier = pltpu.get_barrier_semaphore()
    for device in devices:
        pl.semaphore_signal(barrier, inc=1, device_id=device, device_id_type=MESH)
    pl.semaphore_wait(barrier, len(devices))


def plane_peers():
    s, t = lax.axis_index("seq"), lax.axis_index("tensor")
    return [{"seq": seq_partner(s, k), "tensor": t} for k in (1, 2, 3)] + [
        {"seq": s, "tensor": 1 - t}
    ]


def send(src, dst, send_sem, recv_sem, device):
    copy = pltpu.make_async_remote_copy(
        src_ref=src,
        dst_ref=dst,
        send_sem=send_sem,
        recv_sem=recv_sem,
        device_id=device,
        device_id_type=MESH,
    )
    copy.start()
    return copy


def spread_begin(out_ref, rows, sems):
    s, t = lax.axis_index("seq"), lax.axis_index("tensor")
    mine = out_ref.at[pl.ds(pl.multiple_of((2 * s + t) * rows, rows), rows)]
    devices = [{"seq": s, "tensor": 1 - t}] + [{"seq": seq_partner(s, k), "tensor": t} for k in (1, 2, 3)]
    return [send(mine, mine, sems.at[0, k], sems.at[1, k], devices[k]) for k in (1, 2, 3, 0)]


def spread_end(out_ref, rows, sems, copies):
    s, t = lax.axis_index("seq"), lax.axis_index("tensor")
    for k in (1, 2, 3):
        copies[k - 1].wait_recv()
        came = out_ref.at[pl.ds(pl.multiple_of((2 * seq_partner(s, k) + t) * rows, rows), rows)]
        copies.append(send(came, came, sems.at[0, 3 + k], sems.at[1, 3 + k], {"seq": s, "tensor": 1 - t}))
    for copy in copies[3:]:
        copy.wait_recv()
    for copy in copies:
        copy.wait_send()


def plane_order():
    s = lax.axis_index("seq")
    return [s, seq_partner(s, 1), seq_partner(s, 2), seq_partner(s, 3)]


def sum_begin(part_ref, near_ref, sems):
    s, t = lax.axis_index("seq"), lax.axis_index("tensor")
    to = plane_order()
    return {
        k: send(part_ref.at[to[k], 1 - t], near_ref.at[k], sems.at[0, k], sems.at[1, k], {"seq": s, "tensor": 1 - t})
        for k in (3, 1, 2, 0)
    }


def sum_middle(part_ref, near_ref, low_ref, far_ref, sems, near):
    t = lax.axis_index("tensor")
    to, far = plane_order(), {}
    for k in (3, 1, 2):
        near[k].wait_recv()
        low_ref[k] = (part_ref[to[k], t].astype(F32) + near_ref[k].astype(F32)).astype(LOW)
        far[k] = send(
            low_ref.at[k], far_ref.at[k], sems.at[0, 4 + k], sems.at[1, 4 + k], {"seq": to[k], "tensor": t}
        )
    return far


def sum_end(part_ref, near_ref, far_ref, near, far):
    s, t = lax.axis_index("seq"), lax.axis_index("tensor")
    near[0].wait_recv()
    total = part_ref[s, t].astype(F32) + near_ref[0].astype(F32)
    for k in (1, 2, 3):
        far[k].wait_recv()
        total = total + far_ref[k].astype(F32)
    for copy in (*near.values(), *far.values()):
        copy.wait_send()
    return total


def dot_nt(left, right, precision=None):
    return lax.dot_general(left, right, (((1,), (1,)), ((), ())), precision=precision, preferred_element_type=F32)


def dot_tn(left, right, precision=None):
    return lax.dot_general(left, right, (((0,), (0,)), ((), ())), precision=precision, preferred_element_type=F32)


def dot_nn(left, right, precision=None):
    return lax.dot_general(left, right, (((1,), (0,)), ((), ())), precision=precision, preferred_element_type=F32)


def turn(values, cos_ref, sin_ref):
    return values * cos_ref[...] + pltpu.roll(values, HD // 2, 1) * sin_ref[...]


def turn_back(values, cos_ref, sin_ref):
    return values * cos_ref[...] - pltpu.roll(values, HD // 2, 1) * sin_ref[...]


def visible(col_ref, row_ref):
    return (col_ref[:, 0:1] == row_ref[0:1, :]) & (row_ref[1:2, :] <= col_ref[:, 1:2])


def convolve(mixed, taps_ref, col_ref):
    total = taps_ref[0:1] * mixed
    for lag in range(1, KCONV):
        kept = jnp.where(col_ref[:, 1:2] >= lag, pltpu.roll(mixed, lag, 0), 0.0)
        total = total + taps_ref[lag : lag + 1] * kept
    return total


def steps_and_sums(raw, head_ref, heads, summed=True):
    raw = jnp.where(lax.broadcasted_iota(jnp.int32, raw.shape, 0) < heads, raw, 0.0)
    pre = raw + head_ref[:, 0:1]
    step = jnp.maximum(pre, 0.0) + jnp.log1p(jnp.exp(-jnp.abs(pre)))
    rate = -step * jnp.exp(head_ref[:, 1:2])
    if not summed:
        return pre, step, rate, None
    length = raw.shape[1]
    upto = lax.broadcasted_iota(jnp.int32, (length, length), 0) <= lax.broadcasted_iota(
        jnp.int32, (length, length), 1
    )
    return pre, step, rate, dot_nn(rate, upto.astype(F32), highest)


def when(condition, act):
    if condition is None:
        act()
    else:
        pl.when(condition)(act)


class Moves:
    def __init__(self, dp_count, sems, row, src_of, dst_of, relayed=False):
        d = lax.axis_index("dp")
        self.count, self.sems, self.row, self.d = dp_count, sems, row, d
        self.relayed = relayed and dp_count == 4
        self.copies = {
            k: self.make(src_of(lax.rem(d + k, dp_count)), dst_of(k), k, k, lax.rem(d + k, dp_count))
            for k in range(1, dp_count)
        }

    def make(self, src, dst, at, there, to):
        return pltpu.make_async_remote_copy(
            src_ref=src, dst_ref=dst, send_sem=self.sems.at[self.row, at], recv_sem=self.sems.at[self.row + 1, there],
            device_id={"dp": to}, device_id_type=MESH,
        )

    def direct(self, k):
        if not self.relayed or k == 2:
            return None
        return self.d != (3 if k == 1 else 0)

    def inner(self):
        return (self.d == 1) | (self.d == 2)

    def start(self):
        for k, copy in self.copies.items():
            when(self.direct(k), copy.start)
        return self


class Gather(Moves):
    def __init__(self, dp_count, sems, row, own, full, owner, relayed=True):
        d = lax.axis_index("dp")
        rows = lambda j: full.at[pl.ds(pl.multiple_of(j * owner, owner), owner)]
        super().__init__(dp_count, sems, row, lambda j: own, lambda k: rows(d), relayed)
        if self.relayed:
            far = rows(lax.rem(d + 2, 4))
            self.passed = self.make(far, far, 0, 2 * d - 1, 3 * (d - 1))

    def relay(self):
        if self.relayed:
            def act():
                self.copies[2].wait_recv()
                self.passed.start()

            when(self.inner(), act)

    def finish(self):
        for k, copy in self.copies.items():
            when(jnp.logical_not(self.inner()) if self.relayed and k == 2 else None, copy.wait_recv)

    def wait_send(self):
        for k, copy in self.copies.items():
            when(self.direct(k), copy.wait_send)
        if self.relayed:
            when(self.inner(), self.passed.wait_send)


class Reduce(Moves):
    def __init__(self, dp_count, sems, row, parts, came, owner, relayed=False):
        rows = lambda j: parts.at[pl.ds(pl.multiple_of(j * owner, owner), owner)]
        super().__init__(dp_count, sems, row, rows, lambda k: came.at[k], relayed)
        self.parts, self.came, self.owner = parts, came, owner
        passed = came.at[0]
        if self.relayed:
            self.turns = {1: self.make(rows(0), passed, 1, 0, 2), 3: self.make(rows(3), passed, 3, 0, 1)}

    def start(self):
        if not self.relayed:
            return super().start()
        for k in (1, 3):
            when(jnp.logical_not(self.direct(k)), self.turns[k].start)
        when(self.d == 0, lambda: self.blank(1))
        when(self.d == 3, lambda: self.blank(3))
        when(jnp.logical_not(self.inner()), self.copies[2].start)
        for k in (1, 3):
            when(self.direct(k), self.copies[k].start)
        return self

    def blank(self, k):
        self.came[k] = jnp.zeros(self.came.shape[1:], self.came.dtype)

    def relay(self):
        if self.relayed:
            def act():
                self.turns[1].wait_recv()
                at = pl.ds(pl.multiple_of(lax.rem(self.d + 2, 4) * self.owner, self.owner), self.owner)
                self.parts[at] = (self.parts[at].astype(F32) + self.came[0].astype(F32)).astype(LOW)
                self.copies[2].start()

            when(self.inner(), act)

    def total(self):
        at = pl.ds(pl.multiple_of(self.d * self.owner, self.owner), self.owner)
        value = self.parts[at].astype(F32)
        for k, copy in self.copies.items():
            absent = {1: 0, 3: 3}.get(k)
            when(self.d != absent if self.relayed and absent is not None else None, copy.wait_recv)
        for k in self.copies:
            value = value + self.came[k].astype(F32)
        return value

    def wait_send(self):
        for k, copy in self.copies.items():
            when(self.direct(k), copy.wait_send)
        if self.relayed:
            for k in (1, 3):
                when(jnp.logical_not(self.direct(k)), self.turns[k].wait_send)


class Share(Moves):
    def __init__(self, dp_count, sems, row, own, came):
        super().__init__(dp_count, sems, row, lambda j: own, lambda k: came.at[k])
        self.own, self.came = own, came

    def total(self):
        value = self.own[...]
        for k, copy in self.copies.items():
            copy.wait_recv()
            value = value + self.came[k]
        return value

    def wait_send(self):
        for copy in self.copies.values():
            copy.wait_send()


def convolve_back(grad, mixed, taps_ref, col_ref):
    length = grad.shape[0]
    total = taps_ref[0:1] * grad
    taps = [jnp.sum(grad * mixed, axis=0, keepdims=True)]
    for lag in range(1, KCONV):
        kept = jnp.where(col_ref[:, 1:2] >= lag, grad, 0.0)
        total = total + taps_ref[lag : lag + 1] * pltpu.roll(kept, length - lag, 0)
        taps.append(jnp.sum(kept * pltpu.roll(mixed, lag, 0), axis=0, keepdims=True))
    return total, jnp.concatenate(taps, axis=0)


def norm_backward(grad, values, gain, upstream):
    scale = lax.rsqrt(jnp.mean(values * values, axis=1, keepdims=True) + epsilon)
    normed = values * scale
    grad_gain = jnp.sum(grad * normed, axis=0, keepdims=True)
    inner = grad * gain
    result = upstream + scale * (inner - normed * jnp.mean(inner * normed, axis=1, keepdims=True))
    return result, grad_gain


def silu_slope(pre_act):
    sigmoid_gate = jax.nn.sigmoid(pre_act)
    return sigmoid_gate * (1.0 + pre_act * (1.0 - sigmoid_gate))


def rounded_part(part_ref, value):
    part_ref[...] = value.astype(LOW).reshape(part_ref.shape)


def layer_kernel(
    dp_count, heads,
    spare_ref, hid_all, cot_all, angle_ref, row_ref, conv_ref, head_ref, w_gate, w_in,
    w_query, w_key, w_value, w_bcdt, w_feed_gate, w_feed_up, w_att_out, w_down, w_mamba_out,
    out_ref, hid_grad_ref, fin_feed, fin_outs, fin_entry, fin_x, fin_aux, gains_ref, steps_ref, conv_out, heads_ref,
    entry_own, feed_own, outs_own, outs_rows, col_ref, taps_ref, small_all, gain_all,
    came, tok_ref, feed_ref, low_ref, entry_w, feed_w, outs_w, kv_ref, query_ref, gate_ref, x_ref, step_ref, mixed_ref,
    ssm_ref, prob_ref, decay_ref, meet_ref, middle_ref, grad_ref, dboth_ref, act_ref, back_ref,
    part, near, low, far, gs_feed, gs_outs, gs_entry, gs_x, gs_aux, gr_feed, gr_outs, gr_entry, gr_x, gr_aux,
    aux_send, aux_recv, aux_near, small, small_came, gain, gain_came,
    dp_sem, local, plane_sem, fin_sem, kv_sem, aux_sem, small_sem, gain_sem,
):
    d, s, t = lax.axis_index("dp"), lax.axis_index("seq"), lax.axis_index("tensor")
    rows, owner, width = hid_all.shape[0] // 2, entry_own.shape[0], heads * MP
    length = tok_ref.shape[0]
    other = {"seq": s, "tensor": 1 - t}
    half = act_ref.shape[1]
    cos_ref, sin_ref = angle_ref.at[:, :HD], angle_ref.at[:, HD:]
    own_rows = pl.ds(pl.multiple_of(t * rows, rows), rows)
    hid_ref, cot_ref = hid_all.at[own_rows], cot_all.at[own_rows]

    def lanes_of(weight, size):
        return weight.at[:, pl.ds(pl.multiple_of(s * size, 128), size)]

    def rows_of(weight, size):
        return weight.at[pl.ds(pl.multiple_of(s * size, 64), size)]

    fetches = [
        pltpu.make_async_copy(source, target, local.at[3 + i])
        for i, (source, target) in enumerate(
            (
                (lanes_of(w_query, HD), entry_own.at[:, :HD]),
                (lanes_of(w_feed_gate, half), feed_own.at[:, :half]),
                (lanes_of(w_feed_up, half), feed_own.at[:, half:]),
                (rows_of(w_att_out, HD), outs_rows.at[pl.ds(0, HD)]),
                (rows_of(w_down, half), outs_rows.at[pl.ds(HD, half)]),
                (rows_of(w_mamba_out, width), outs_rows.at[pl.ds(HD + half, width)]),
            )
        )
    ]
    for copy in fetches:
        copy.start()
    for i, source in enumerate((w_key, w_value, w_bcdt.at[:, :NS], w_bcdt.at[:, NS : 2 * NS])):
        def columns_of(i=i, source=source):
            copy = pltpu.make_async_copy(source, entry_own.at[:, HD : 2 * HD], local.at[9])
            copy.start()
            entry_own[:, 2 * HD : 2 * HD + width] = w_gate[:, i * width : (i + 1) * width]
            entry_own[:, 2 * HD + width :] = w_in[:, i * width : (i + 1) * width]
            for j in range(2):
                def taps_of(j=j):
                    g = 4 * j + i
                    taps_ref[:, 2 * NS :] = conv_ref[:, g * width : (g + 1) * width]

                pl.when(t == j)(taps_of)
            copy.wait()

        pl.when(s == i)(columns_of)
    taps_ref[:, : 2 * NS] = conv_ref[:, MD:]
    col_ref[...] = row_ref[...].T
    peers = []
    for k in range(4):
        for flip in range(2):
            if k or flip:
                peers.append({"seq": s if k == 0 else seq_partner(s, k), "tensor": 1 - t if flip else t})
    seq_peers = [{"seq": seq_partner(s, k), "tensor": t} for k in (1, 2, 3)]
    greet(peers + [{"dp": lax.rem(d + k, dp_count)} for k in range(1, dp_count)])
    place = pl.ds(pl.multiple_of(d * owner, owner), owner)
    spares = Share(dp_count, dp_sem, 0, spare_ref, came).start()
    fetches[0].wait()
    entries = Gather(dp_count, dp_sem, 2, entry_own, entry_w, owner).start()
    locals_ = [
        pltpu.make_async_copy(own, full.at[place], local.at[i])
        for i, (own, full) in enumerate(((entry_own, entry_w), (feed_own, feed_w), (outs_own, outs_w)))
    ]
    locals_[0].start()
    hid = hid_ref[...]
    normed = hid * lax.rsqrt(jnp.mean(hid * hid, axis=1, keepdims=True) + epsilon)
    total = spares.total()
    gain_one, gain_two, step_w = total[3:4], total[4:5], total.astype(LOW)
    mine = pl.ds(pl.multiple_of((2 * s + t) * rows, rows), rows)
    tok_ref[mine, :D] = (normed * gain_one).astype(LOW)
    tok_ref[mine, D:] = cot_ref[...].astype(LOW)
    spread_end(tok_ref, rows, plane_sem.at[0], spread_begin(tok_ref, rows, plane_sem.at[0]))
    for copy in fetches[1:]:
        copy.wait()
    unit = (
        lax.broadcasted_iota(jnp.int32, (owner, owner), 0) == lax.broadcasted_iota(jnp.int32, (owner, owner), 1)
    ).astype(F32).astype(LOW)
    outs_own[...] = dot_nt(unit, outs_rows[...]).astype(LOW)
    for copy in locals_[1:]:
        copy.start()
    entries.relay()
    outers = Gather(dp_count, dp_sem, 4, outs_own, outs_w, owner).start()
    entries.finish()
    feeds = Gather(dp_count, dp_sem, 6, feed_own, feed_w, owner).start()
    for copy in locals_:
        copy.wait()

    mixer_in = tok_ref[:, :D]
    aux = dot_nn(mixer_in, entry_w[:, HD : 2 * HD])
    is_key = jnp.where(s == 0, 1.0, 0.0)
    aux = turn(aux, cos_ref, sin_ref) * is_key + aux * (1.0 - is_key)
    kv_ref[s] = aux.astype(LOW)
    shared = [
        send(kv_ref.at[s], kv_ref.at[s], kv_sem.at[0, i], kv_sem.at[1, i], peer)
        for i, peer in enumerate(seq_peers)
    ]
    query_ref[...] = turn(dot_nn(mixer_in, entry_w[:, :HD]), cos_ref, sin_ref).astype(LOW)
    gate_x = dot_nn(mixer_in, entry_w[:, 2 * HD :])
    gate_ref[...] = gate_x[:, :width]
    x_ref[...] = gate_x[:, width:].astype(LOW)
    step_ref[...] = dot_nt(step_w, mixer_in).astype(LOW).astype(F32)
    _, step, _, cum = steps_and_sums(step_ref[...], head_ref, heads)
    columns = jnp.concatenate([cum, step], axis=0).T
    cum_col, step_col = columns[:, :8], columns[:, 8:]
    x_conv = convolve(x_ref[...].astype(F32), taps_ref.at[:, 2 * NS :], col_ref)
    x_act = x_conv * jax.nn.sigmoid(x_conv)
    allowed = visible(col_ref, row_ref)
    for copy in shared:
        copy.wait_recv()

    scores = jnp.where(allowed, dot_nt(query_ref[...], kv_ref[0]) * HD ** (-0.5), masked_score)
    peak = jnp.max(scores, axis=1, keepdims=True)
    logsum = peak + jnp.log(jnp.sum(jnp.exp(scores - peak), axis=1, keepdims=True))
    probs = jnp.exp(scores - logsum)
    prob_ref[...] = probs
    mixed_ref[:, :HD] = dot_nn(probs.astype(LOW), kv_ref[1]).astype(LOW)

    outers.relay()

    def state(index):
        conv = convolve(kv_ref[2 + index].astype(F32), taps_ref.at[:, index * NS : (index + 1) * NS], col_ref)
        return conv

    bconv, cconv = state(0), state(1)
    bstate, cstate = bconv * jax.nn.sigmoid(bconv), cconv * jax.nn.sigmoid(cconv)
    meet_ref[...] = dot_nt(cstate, bstate, highest)
    sums = []
    for h in range(heads):
        decay = jnp.exp(jnp.where(allowed, cum_col[:, h : h + 1] - cum[h : h + 1, :], masked_score))
        decay_ref[h] = decay
        x_head = x_act[:, h * MP : (h + 1) * MP]
        sums.append(dot_nn(meet_ref[...] * decay, x_head * step_col[:, h : h + 1], highest))
    core_out = jnp.concatenate(sums, axis=1)
    skips = jnp.concatenate(
        [jnp.broadcast_to(head_ref[h : h + 1, 2:3], (1, MP)) for h in range(heads)], axis=1
    )
    ssm_ref[...] = core_out
    ssm_low = (core_out + skips * x_act).astype(LOW).astype(F32)
    gate_pre = gate_ref[...]
    mixed_ref[:, HD:] = (ssm_low * (gate_pre * jax.nn.sigmoid(gate_pre))).astype(LOW)

    outers.finish()
    down_start = HD + act_ref.shape[1]
    rounded_part(
        part.at[0],
        dot_nt(mixed_ref[:, :HD], outs_w[:, :HD]) + dot_nt(mixed_ref[:, HD:], outs_w[:, down_start:]),
    )

    def begin(i):
        return sum_begin(part.at[i % 3], near.at[i % 3], plane_sem.at[1 + i])

    def middle_of(i, copies):
        return sum_middle(part.at[i % 3], near.at[i % 3], low.at[i % 3], far.at[i % 3], plane_sem.at[1 + i], copies)

    def end(i, copies, later):
        return sum_end(part.at[i % 3], near.at[i % 3], far.at[i % 3], copies, later)

    sum_near = begin(0)
    feeds.relay()
    middle = hid_ref[...] + end(0, sum_near, middle_of(0, sum_near))
    middle_ref[...] = middle
    scale = lax.rsqrt(jnp.mean(middle * middle, axis=1, keepdims=True) + epsilon)
    feed_ref[mine, :] = (middle * scale * gain_two).astype(LOW)
    spread_end(feed_ref, rows, plane_sem.at[5], spread_begin(feed_ref, rows, plane_sem.at[5]))
    feeds.finish()

    feed_gate = dot_nn(feed_ref[...], feed_w[:, :half])
    feed_up = dot_nn(feed_ref[...], feed_w[:, half:])
    feed_sig = jax.nn.sigmoid(feed_gate)
    feed_silu = feed_gate * feed_sig
    act_ref[...] = (feed_silu * feed_up).astype(LOW)
    grad_act = dot_nn(tok_ref[:, D:], outs_w[:, HD:down_start])
    dboth_ref[:, :half] = (grad_act * feed_up * (feed_sig * (1.0 + feed_gate * (1.0 - feed_sig)))).astype(LOW)
    dboth_ref[:, half:] = (grad_act * feed_silu).astype(LOW)
    rounded_part(part.at[1], dot_nt(dboth_ref[...], feed_w[...]))
    sum_near = begin(1)
    gs_feed[:, : 2 * half] = dot_tn(feed_ref[...], dboth_ref[...]).astype(LOW)
    sum_far = middle_of(1, sum_near)
    gs_feed[:, 2 * half :] = dot_tn(tok_ref[:, D:], act_ref[...]).astype(LOW)

    def publish(reduce, fin, row):
        fin[s] = reduce.total().astype(LOW)
        return [
            send(fin.at[s], fin.at[s], fin_sem.at[row, 0, i], fin_sem.at[row, 1, i], peer)
            for i, peer in enumerate(seq_peers)
        ]

    feed_red = Reduce(dp_count, dp_sem, 8, gs_feed, gr_feed, owner, True).start()
    grad_middle, grad_gain_two = norm_backward(end(1, sum_near, sum_far), middle_ref[...], gain_two, cot_ref[...])
    grad_ref[...] = grad_middle
    low_ref[mine, :] = grad_middle.astype(LOW)
    spread = spread_begin(low_ref, rows, plane_sem.at[6])
    rounded_part(part.at[2], dot_nt(act_ref[...], outs_w[:, HD:down_start]))
    spread_end(low_ref, rows, plane_sem.at[6], spread)
    out_near = begin(2)

    grad_gated = dot_nn(low_ref[...], outs_w[:, down_start:])
    grad_attended = dot_nn(low_ref[...], outs_w[:, :HD]).astype(LOW)
    gs_outs[...] = dot_tn(low_ref[...], mixed_ref[...]).astype(LOW)
    outs_red = Reduce(dp_count, dp_sem, 10, gs_outs, gr_outs, owner, True).start()
    gate_sig = jax.nn.sigmoid(gate_pre)
    back_ref[:, HD : HD + width] = (
        grad_gated * ssm_low * (gate_sig * (1.0 + gate_pre * (1.0 - gate_sig)))
    ).astype(LOW)
    dy = (grad_gated * (gate_pre * gate_sig)).astype(LOW).astype(F32)

    row_delta = jnp.sum(grad_attended.astype(F32) * mixed_ref[:, :HD].astype(F32), axis=1, keepdims=True)
    probs = prob_ref[...]
    aux_send[1] = dot_tn(probs.astype(LOW), grad_attended).astype(LOW)
    dscores = (probs * (dot_nt(grad_attended, kv_ref[1]) - row_delta)).astype(LOW)
    back_ref[:, :HD] = turn_back(dot_nn(dscores, kv_ref[0]) * HD ** (-0.5), cos_ref, sin_ref).astype(LOW)
    aux_send[0] = turn_back(dot_tn(dscores, query_ref[...]) * HD ** (-0.5), cos_ref, sin_ref).astype(LOW)
    out_far = middle_of(2, out_near)
    gs_entry[...] = dot_tn(mixer_in, back_ref[:, : HD + width]).astype(LOW)
    entry_red = Reduce(dp_count, dp_sem, 12, gs_entry, gr_entry, owner, True).start()
    feed_red.relay()

    dmeet = jnp.zeros((length, length), F32)
    dx_parts, dcum_cols, dstep_cols, dskips = [], [], [], []
    for h in range(heads):
        cols = slice(h * MP, (h + 1) * MP)
        step_h = step_col[:, h : h + 1]
        dy_h, x_h = dy[:, cols], x_act[:, cols]
        u_h = x_h * step_h
        du = dot_tn(meet_ref[...] * decay_ref[h], dy_h, highest)
        dmeet = dmeet + dot_nt(dy_h, u_h, highest) * decay_ref[h]
        dx_parts.append(du * step_h + head_ref[h : h + 1, 2:3] * dy_h)
        dstep_cols.append(jnp.sum(x_h * du, axis=1, keepdims=True))
        dcum_cols.append(jnp.sum(dy_h * ssm_ref[:, cols] - u_h * du, axis=1, keepdims=True))
        dskips.append(jnp.sum(jnp.sum(dy_h * x_h, axis=1, keepdims=True), axis=0, keepdims=True))
    dx_act = jnp.concatenate(dx_parts, axis=1)
    outs_red.relay()
    finals = publish(feed_red, fin_feed, 0)
    blank = jnp.zeros((length, 1), F32)
    flat = jnp.concatenate(
        dcum_cols + [blank] * (8 - heads) + dstep_cols + [blank] * (8 - heads), axis=1
    ).T
    dcum, dstep = flat[:8], flat[8:]
    at_least = lax.broadcasted_iota(jnp.int32, (length, length), 0) >= lax.broadcasted_iota(
        jnp.int32, (length, length), 1
    )
    drate = dot_nn(dcum, at_least.astype(F32), highest)
    pre, step, rate, _ = steps_and_sums(step_ref[...], head_ref, heads, False)
    dpre = (dstep - drate * jnp.exp(head_ref[:, 1:2])) * jax.nn.sigmoid(pre)
    dstep_low = dpre.astype(LOW)
    small[...] = jnp.zeros_like(small)
    small[0:1, :] = grad_gain_two
    small[1 : 1 + heads, :] = dot_nn(dstep_low, mixer_in)[:heads]
    head_row = 1 + heads + KCONV
    small[head_row : head_row + heads, 0:128] = jnp.broadcast_to(
        jnp.sum(drate * rate, axis=1, keepdims=True)[:heads], (heads, 128)
    )
    small[head_row : head_row + heads, 128:256] = jnp.broadcast_to(
        jnp.sum(dpre, axis=1, keepdims=True)[:heads], (heads, 128)
    )
    small[head_row : head_row + heads, 256:384] = jnp.broadcast_to(jnp.concatenate(dskips, axis=0), (heads, 128))

    dconv = dx_act * silu_slope(x_conv)
    dx, dtaps = convolve_back(dconv, x_ref[...].astype(F32), taps_ref.at[:, 2 * NS :], col_ref)
    back_ref[:, HD + width :] = dx.astype(LOW)
    small[1 + heads : head_row, 2 * NS : 2 * NS + width] = dtaps
    for index, grad, conv in (
        (0, dot_tn(dmeet, cstate, highest), bconv),
        (1, dot_nn(dmeet, bstate, highest), cconv),
    ):
        lanes = slice(index * NS, (index + 1) * NS)
        grad_in, dtaps = convolve_back(
            grad * silu_slope(conv), kv_ref[2 + index].astype(F32), taps_ref.at[:, lanes], col_ref
        )
        aux_send[2 + index] = grad_in.astype(LOW)
        small[1 + heads : head_row, lanes] = dtaps

    to = plane_order()
    aux_copies = [
        send(aux_send.at[to[k]], aux_recv.at[k], aux_sem.at[0, k], aux_sem.at[1, k], seq_peers[k - 1])
        for k in (1, 2, 3)
    ]
    small_dp = Share(dp_count, dp_sem, 16, small, small_came).start()
    gs_x[...] = dot_tn(mixer_in, back_ref[:, HD + width :]).astype(LOW)
    x_red = Reduce(dp_count, dp_sem, 20, gs_x, gr_x, owner).start()
    entry_red.relay()
    finals += publish(outs_red, fin_outs, 1)
    aux_sum = aux_send[s].astype(F32)
    for k in (1, 2, 3):
        aux_copies[k - 1].wait_recv()
        aux_sum = aux_sum + aux_recv[k].astype(F32)
    aux_near[0] = aux_sum.astype(LOW)
    pair = send(aux_near.at[0], aux_near.at[1], aux_sem.at[0, 0], aux_sem.at[1, 0], other)
    input_part = (
        dot_nt(back_ref[:, :HD], entry_w[:, :HD])
        + dot_nt(back_ref[:, HD:], entry_w[:, 2 * HD :])
        + dot_tn(dstep_low, step_w)
    )
    both = jnp.where(s >= 2, 1.0, 0.0)
    once = jnp.where(t == 0, 1.0, 1.0 - both)
    pair.wait_recv()
    daux = (aux_sum + both * aux_near[1].astype(F32)).astype(LOW)
    daux_once = (daux.astype(F32) * once).astype(LOW)
    rounded_part(part.at[0], input_part + dot_nt(daux_once, entry_w[:, HD : 2 * HD]))
    in_near = begin(3)
    gs_aux[...] = dot_tn(mixer_in, daux).astype(LOW)
    aux_red = Reduce(dp_count, dp_sem, 14, gs_aux, gr_aux, owner).start()
    in_far = middle_of(3, in_near)

    out_ref[t] = middle_ref[...] + end(2, out_near, out_far)
    out_pair = send(out_ref.at[t], out_ref.at[t], kv_sem.at[0, 3], kv_sem.at[1, 3], other)
    index = 2 * s + t
    small_all[index] = small_dp.total()
    small_plane = [
        send(small_all.at[index], small_all.at[index], small_sem.at[0, i], small_sem.at[1, i], peer)
        for i, peer in enumerate(peers)
    ]
    grad_hidden, grad_gain_one = norm_backward(end(3, in_near, in_far), hid_ref[...], gain_one, grad_ref[...])
    hid_grad_ref[t] = grad_hidden
    hid_pair = send(hid_grad_ref.at[t], hid_grad_ref.at[t], aux_sem.at[0, 4], aux_sem.at[1, 4], other)
    gain[...] = jnp.broadcast_to(grad_gain_one, gain.shape)
    gain_dp = Share(dp_count, dp_sem, 18, gain, gain_came).start()
    finals += publish(entry_red, fin_entry, 2)
    gain_all[index] = gain_dp.total()
    gain_plane = [
        send(gain_all.at[index], gain_all.at[index], gain_sem.at[0, i], gain_sem.at[1, i], peer)
        for i, peer in enumerate(peers)
    ]
    finals += publish(x_red, fin_x, 3)
    finals += publish(aux_red, fin_aux, 4)
    for copy in (*small_plane, *gain_plane):
        copy.wait_recv()
        copy.wait_send()
    summed = small_all[0]
    for i in range(1, 8):
        summed = summed + small_all[i]
    gain_sum = gain_all[0, 0:1]
    for i in range(1, 8):
        gain_sum = gain_sum + gain_all[i, 0:1]
    gains_ref[0:1, :] = gain_sum
    gains_ref[1:2, :] = summed[0:1]
    conv_out[:, MD:] = summed[1 + heads : head_row, : 2 * NS]
    for g in range(8):
        slot = 2 * (g % 4) + g // 4
        steps_ref[g * heads : (g + 1) * heads, :] = small_all[slot, 1 : 1 + heads, :]
        conv_out[:, g * width : (g + 1) * width] = small_all[slot, 1 + heads : head_row, 2 * NS : 2 * NS + width]
        heads_ref[g * heads : (g + 1) * heads, :] = small_all[slot, head_row : head_row + heads, : 3 * 128]
    for copy in (out_pair, hid_pair, *finals):
        copy.wait_recv()
        copy.wait_send()
    for copy in (
        spares, entries, outers, feeds, *shared, feed_red, outs_red, entry_red, x_red, aux_red, *aux_copies, pair,
        small_dp, gain_dp,
    ):
        copy.wait_send()


def call(kernel, collective_id, outs, scratch, *operands, far=()):
    vmem = pl.BlockSpec(memory_space=pltpu.VMEM)
    in_specs = [pl.BlockSpec(memory_space=pl.ANY) if i in far else vmem for i in range(len(operands))]
    return pl.pallas_call(
        kernel,
        out_shape=[jax.ShapeDtypeStruct(shape, kind) for shape, kind in outs],
        in_specs=in_specs,
        out_specs=[vmem] * len(outs),
        scratch_shapes=scratch,
        compiler_params=pltpu.CompilerParams(
            collective_id=collective_id, has_side_effects=True, vmem_limit_bytes=60 * 2**20
        ),
    )(*operands)


def dma_sems(*counts):
    return [pltpu.SemaphoreType.DMA((count,)) for count in counts]


def body(
    hidden_in,
    cotangent,
    segment_ids,
    positions,
    w_query,
    w_key,
    w_value,
    w_mamba_gate,
    w_mamba_in,
    w_mamba_bcdt,
    w_attention_out,
    w_mamba_out,
    w_feed_gate,
    w_feed_up,
    w_feed_down,
    gain_mixer,
    gain_feed,
    conv_weight,
    log_decay,
    step_bias,
    skip_scale,
):
    s, t, d = lax.axis_index("seq"), lax.axis_index("tensor"), lax.axis_index("dp")
    seq_count, tensor_count, dp_count = (
        lax.axis_size("seq"),
        lax.axis_size("tensor"),
        lax.axis_size("dp"),
    )
    length = segment_ids.shape[0]
    rows = hidden_in.shape[0] // tensor_count
    owner = w_query.shape[0]
    heads_dev = MH // (seq_count * tensor_count)
    width = heads_dev * MP
    group = t * seq_count + s
    score_scale = HD ** (-0.5)
    feed_width = w_feed_gate.shape[1] // seq_count

    step_cols = lax.dynamic_slice_in_dim(w_mamba_bcdt, 2 * NS + group * heads_dev, heads_dev, 1)
    spare = jnp.concatenate(
        [step_cols.T, gain_mixer[None], gain_feed[None], jnp.zeros((6 - heads_dev, owner), LOW)], axis=0
    ).astype(F32)
    lane = lax.broadcasted_iota(jnp.int32, (8, D), 1)
    spare = jnp.where(lane // owner == d, jnp.tile(spare, (1, dp_count)), 0.0)
    lane = lax.broadcasted_iota(jnp.int32, (length, 2 * HD), 1)
    freq = jnp.exp((lane % (HD // 2)).astype(F32) * (-2.0 * math.log(rope_base) / HD))
    angle = positions.astype(F32)[:, None] * freq
    sine = jnp.sin(angle)
    angles = jnp.where(lane < HD, jnp.cos(angle), jnp.where(lane < HD + HD // 2, -sine, sine))
    row_meta = jnp.pad(jnp.stack([segment_ids, positions]), ((0, 6), (0, 0))).astype(F32)
    head_meta = lax.dynamic_slice_in_dim(
        jnp.pad(jnp.stack([step_bias, log_decay, skip_scale], axis=1), ((0, 8), (0, 125))), group * heads_dev, 8, 0
    )
    n = dp_count
    vmem, total_rows = pltpu.VMEM, seq_count * tensor_count * rows
    sizes = (3 * feed_width, HD + width, HD + width, width, HD)
    out_two, hid_two, fin_feed, fin_outs, fin_entry, fin_x, fin_aux, gains, steps, grad_conv_weight, heads = call(
        functools.partial(layer_kernel, dp_count, heads_dev),
        1,
        [
            ((2, rows, D), F32),
            ((2, rows, D), F32),
            *[((seq_count, owner, size), LOW) for size in sizes],
            ((2, D), F32),
            ((MH, D), F32),
            (conv_weight.shape, F32),
            ((MH, 384), F32),
        ],
        [
            vmem((owner, 2 * HD + 2 * width), LOW),
            vmem((owner, 2 * feed_width), LOW),
            vmem((owner, HD + width + feed_width), LOW),
            vmem((HD + width + feed_width, owner), LOW),
            vmem((length, 8), F32),
            vmem((KCONV, 2 * NS + width), F32),
            vmem((8, 16, D), F32),
            vmem((8, 8, D), F32),
            vmem((n, 8, D), F32),
            vmem((length, 2 * D), LOW),
            vmem((length, D), LOW),
            vmem((length, D), LOW),
            vmem((D, 2 * HD + 2 * width), LOW),
            vmem((D, 2 * feed_width), LOW),
            vmem((D, HD + width + feed_width), LOW),
            vmem((seq_count, length, HD), LOW),
            vmem((length, HD), LOW),
            vmem((length, width), F32),
            vmem((length, width), LOW),
            vmem((8, length), F32),
            vmem((length, HD + width), LOW),
            vmem((length, width), F32),
            vmem((length, length), F32),
            vmem((heads_dev, length, length), F32),
            vmem((length, length), F32),
            vmem((rows, D), F32),
            vmem((rows, D), F32),
            vmem((length, 2 * feed_width), LOW),
            vmem((length, feed_width), LOW),
            vmem((length, HD + 2 * width), LOW),
            vmem((3, seq_count, tensor_count, rows, D), LOW),
            *[vmem((3, 4, rows, D), LOW) for _ in range(3)],
            *[vmem((D, size), LOW) for size in sizes],
            *[vmem((n, owner, size), LOW) for size in sizes],
            vmem((seq_count, length, HD), LOW),
            vmem((4, length, HD), LOW),
            vmem((2, length, HD), LOW),
            vmem((16, D), F32),
            vmem((n, 16, D), F32),
            vmem((8, D), F32),
            vmem((n, 8, D), F32),
            pltpu.SemaphoreType.DMA((22, n)),
            pltpu.SemaphoreType.DMA((10,)),
            pltpu.SemaphoreType.DMA((7, 2, 8)),
            pltpu.SemaphoreType.DMA((5, 2, 3)),
            pltpu.SemaphoreType.DMA((2, 4)),
            pltpu.SemaphoreType.DMA((2, 5)),
            pltpu.SemaphoreType.DMA((2, 7)),
            pltpu.SemaphoreType.DMA((2, 7)),
        ],
        spare, hidden_in, cotangent, angles, row_meta, conv_weight, head_meta, w_mamba_gate, w_mamba_in,
        w_query, w_key, w_value, w_mamba_bcdt, w_feed_gate, w_feed_up, w_attention_out, w_feed_down, w_mamba_out,
        far=range(9, 18),
    )
    output, grad_hidden = out_two.reshape(2 * rows, D), hid_two.reshape(2 * rows, D)

    gains = lax.dynamic_slice_in_dim(gains, d * owner, owner, 1)
    grad_step_w = lax.dynamic_slice_in_dim(steps, d * owner, owner, 1).T

    side = lambda blocks, low, high: jnp.concatenate(
        [blocks[i, :, low:high].astype(F32) for i in range(seq_count)], axis=1
    )
    below = lambda blocks, low, high: jnp.concatenate(
        [blocks[i, :, low:high].astype(F32).T for i in range(seq_count)], axis=0
    )
    return (
        output,
        grad_hidden,
        side(fin_entry, 0, HD),
        fin_aux[0].astype(F32),
        fin_aux[1].astype(F32),
        side(fin_entry, HD, HD + width),
        side(fin_x, 0, width),
        jnp.concatenate([fin_aux[2].astype(F32), fin_aux[3].astype(F32), grad_step_w], axis=1),
        below(fin_outs, 0, HD),
        below(fin_outs, HD, HD + width),
        side(fin_feed, 0, feed_width),
        side(fin_feed, feed_width, 2 * feed_width),
        below(fin_feed, 2 * feed_width, 3 * feed_width),
        gains[0],
        gains[1],
        grad_conv_weight,
        heads[:, 0],
        heads[:, 128],
        heads[:, 256],
    )


def solution(mesh):
    return jax.shard_map(
        body,
        mesh=mesh,
        in_specs=(
            P(("dp", "seq"), None),
            P(("dp", "seq"), None),
            P("dp"),
            P("dp"),
            P("dp", "tensor"),
            P("dp", "tensor"),
            P("dp", "tensor"),
            P("dp", "tensor"),
            P("dp", "tensor"),
            P("dp", None),
            P("tensor", "dp"),
            P("tensor", "dp"),
            P("dp", "tensor"),
            P("dp", "tensor"),
            P("tensor", "dp"),
            P("dp"),
            P("dp"),
            P(),
            P(),
            P(),
            P(),
        ),
        out_specs=(
            P(("dp", "seq"), None),
            P(("dp", "seq"), None),
            P("dp", "tensor"),
            P("dp", "tensor"),
            P("dp", "tensor"),
            P("dp", "tensor"),
            P("dp", "tensor"),
            P("dp", None),
            P("tensor", "dp"),
            P("tensor", "dp"),
            P("dp", "tensor"),
            P("dp", "tensor"),
            P("tensor", "dp"),
            P("dp"),
            P("dp"),
            P(),
            P(),
            P(),
            P(),
        ),
        check_vma=False,
    )
```
